32 devices in a mesh: lon: 8 (over z, x), lat: 4 (over y, core).
Axes of the slice: x: 2, y: 2, z: 4, core: 2. Of those that a mesh axis runs over, the one named last changes fastest.
Arguments:
- inputs: bfloat16 [256, 32, 2048], P(None, 'lat', 'lon'), may hold values from -6 to 6
- cotangent: bfloat16 [256, 32, 2048], P(None, 'lat', 'lon'), may hold values from -6 to 6
- mixing: bfloat16 [9, 256, 256], replicated, may hold values from -0.125 to 0.125
- filters: bfloat16 [9, 32, 3, 33], P(None, 'lat'), may hold values from -0.8984375 to 0.8984375
- support: int32 [32], P('lat'), may hold values from 1 to 16, as said below
Outputs:
- input_grad: bfloat16 [256, 32, 2048], P(None, 'lat', 'lon')
- weight_grad: float32 [9, 256, 256], replicated
The draws below stay inside these ranges and needn't reach their ends.
Inputs may be any that keep to these rules, and one draw needn't show every extreme that they name: support[i] is the widest longitude offset, in cells, reached by the filter of latitude row i.
All inputs are finite; a program needn't handle non-finite values.
Results may differ from the reference program's by a relative error of at most 0.0051.
Values may be sent and summed in bfloat16 or wider, within the bound.
A program may use at most 192 MiB of HBM per device.

```python
import math
import jax
import jax.numpy as jnp
from jax import lax

CHANNELS = 256
KERNELS = 9
LAT_REACH = 1
LON_REACH = 16
NLAT = 32
NLON = 2048


def draw_support(key, part):
    first_key, second_key, third_key = jax.random.split(key, 3)
    rows = jnp.arange(NLAT, dtype=jnp.int32)
    distance = jnp.abs(2 * rows + 1 - NLAT)
    base_width = 1 + (LON_REACH - 4) * distance * distance // (NLAT * NLAT)
    jitter = jax.random.randint(first_key, (NLAT,), 0, 4, dtype=jnp.int32)
    widths = jnp.minimum(base_width + jitter, LON_REACH)
    widest = jax.random.randint(second_key, (), 0, NLAT, dtype=jnp.int32)
    narrow = (widest + 1 + jax.random.randint(third_key, (), 0, NLAT - 1, dtype=jnp.int32)) % NLAT
    widths = widths.at[widest].set(LON_REACH)
    widths = widths.at[narrow].set(1)
    return widths.astype(jnp.int32)


def shard_levels(own_key, shape, pieces, smallest, largest):
    gain, own = 1.0, jax.random.fold_in(own_key, 6)
    for dim, shards_of in pieces:
        heights = jnp.exp(jax.random.uniform(jax.random.fold_in(own, dim), (shards_of,), jnp.float32, smallest / len(pieces), largest / len(pieces)))
        gain = gain * jnp.repeat(heights, shape[dim] // shards_of).reshape([-1 if axis == dim else 1 for axis in range(len(shape))])
    return gain


def noise(rng, extent, deviation, limit, shards=(), kind=jnp.bfloat16):
    factor_of = shard_levels(rng, extent, shards, -0.22, 0.18) if shards else 1.0
    array = jax.random.normal(rng, extent, jnp.float32) * deviation * factor_of
    return jnp.minimum(jnp.maximum(array, -limit), limit).astype(kind)


def setup_inputs(seed: int = 0) -> dict:
    key_of = jax.random.split(jax.random.key(seed), 6)
    inputs = noise(key_of[0], (CHANNELS, NLAT, NLON), 1.0, 6.0, ((1, 4), (2, 8)))
    cotangent = noise(key_of[1], (CHANNELS, NLAT, NLON), 1.0, 6.0, ((1, 4), (2, 8)))
    mixing = noise(key_of[2], (KERNELS, CHANNELS, CHANNELS), (KERNELS * CHANNELS) ** -0.5, 0.125)
    filters = noise(key_of[3], (KERNELS, NLAT, 2 * LAT_REACH + 1, 2 * LON_REACH + 1), 0.15, 0.8984375, ((1, 4),))
    support = draw_support(jax.random.fold_in(key_of[5], 71), 0)
    return {"inputs": inputs, "cotangent": cotangent, "mixing": mixing, "filters": filters, "support": support}


def masked_filters(filters, support):
    offsets = jnp.arange(2 * LON_REACH + 1, dtype=jnp.int32) - LON_REACH
    keep = (jnp.abs(offsets)[None, :] <= support[:, None]).astype(jnp.bfloat16)
    return filters * keep[None, :, None, :]

def wrap_pad(field, row_axis):
    widths = [(0, 0)] * field.ndim
    widths[row_axis] = (LAT_REACH, LAT_REACH)
    padded = jnp.pad(field, widths)
    return jnp.concatenate([padded[..., NLON - LON_REACH:], padded, padded[..., :LON_REACH]], axis=-1)

def reference(inputs, cotangent, mixing, filters, support):
    coefs = masked_filters(filters, support)
    cot_pad = wrap_pad(cotangent, 1)
    coef_pad = jnp.pad(coefs, ((0, 0), (LAT_REACH, LAT_REACH), (0, 0), (0, 0)))
    mix_wide = mixing.astype(jnp.float32)
    tap_count = 2 * LON_REACH + 1
    band_rows = 2 * LAT_REACH + 1

    def row_step(grad_acc, row_index):
        total = jnp.zeros((KERNELS, CHANNELS, NLON), jnp.float32)
        for offset in range(band_rows):
            source = row_index - offset + 2 * LAT_REACH
            cot_row = lax.dynamic_index_in_dim(cot_pad, source, 1, False).astype(jnp.float32)
            row_coefs = lax.dynamic_index_in_dim(coef_pad, source, 1, False)[:, offset, :].astype(jnp.float32)
            windows = jnp.stack([cot_row[:, 2 * LON_REACH - shift_col:2 * LON_REACH - shift_col + NLON] for shift_col in range(tap_count)], -1)
            total = total + jnp.einsum('cwb,kb->kcw', windows, row_coefs)
        spread = total.astype(jnp.bfloat16)
        spread = lax.optimization_barrier(spread).astype(jnp.float32)
        input_row = lax.dynamic_index_in_dim(inputs, row_index, 1, False).astype(jnp.float32)
        grad_acc = grad_acc + jnp.einsum('kow,cw->koc', spread, input_row)
        grad_row = jnp.einsum('koc,kow->cw', mix_wide, spread).astype(jnp.bfloat16)
        return (grad_acc, grad_row)
    weight_grad, rows = lax.scan(row_step, jnp.zeros((KERNELS, CHANNELS, CHANNELS), jnp.float32), jnp.arange(NLAT, dtype=jnp.int32))
    weight_grad = weight_grad * (1.0 / math.sqrt(NLAT * NLON))
    input_grad = jnp.transpose(rows, (1, 0, 2))
    return (input_grad, weight_grad)
```

```python
import functools
import math

import jax
import jax.numpy as jnp
from jax import lax
from jax.experimental import pallas as pl
from jax.experimental.pallas import tpu as pltpu
from jax.sharding import PartitionSpec as P

LAT_REACH = 1
LON_REACH = 16
TAPS = 2 * LON_REACH + 1
ROWS_A = 2 * LAT_REACH + 1
BLOCK = 48
WINDOW = BLOCK + 2 * LON_REACH
DEPTH = 256
TILE = 16
LANES = 128
GROUPS = 3

F32 = jnp.float32
BF16 = jnp.bfloat16
MESH = pl.DeviceIdType.MESH


def nt_dot(a, b):
    return lax.dot_general(a, b, (((1,), (1,)), ((), ())), preferred_element_type=F32)


def nn_dot(a, b):
    return lax.dot_general(a, b, (((1,), (0,)), ((), ())), preferred_element_type=F32)


def flip(index, step):
    return index + step - 2 * step * ((index // step) % 2)


def stage_orders(nlon, nlat):
    lat_bits = [("lat", 2**i) for i in range(1, nlat.bit_length() - 1)]
    lon_bits = [("lon", 2**i) for i in range(nlon.bit_length() - 1)]
    first, second = [], []
    for i in range(max(len(lat_bits), len(lon_bits))):
        first += lon_bits[i : i + 1] + lat_bits[i : i + 1]
        second += lat_bits[i : i + 1] + lon_bits[i : i + 1]
    return first, second


def kernel(
    nlon, nlat, kernels, chans, rows, cols,
    cot_hbm, inp_hbm, mix_hbm, taps_hbm, ig_hbm, wg_hbm,
    cot_v, inp_v, mix_v, taps_v, by_row, inp_r, cot_t, toep, spread, acc, snd0, rcv0,
    accs, snds, rcvs, gat, wg_v, ig_row, ig_v,
    in_sem, out_sem, halo_send, halo_recv, ar_send, ar_recv,
):
    lon, lat = lax.axis_index("lon"), lax.axis_index("lat")
    core = lat % 2
    first, second = stage_orders(nlon, nlat)
    per = kernels // GROUPS

    loads = [
        pltpu.make_async_copy(cot_hbm, cot_v, in_sem.at[0]),
        pltpu.make_async_copy(taps_hbm, taps_v.at[:, pl.ds(1, rows)], in_sem.at[1]),
        pltpu.make_async_copy(inp_hbm, inp_v, in_sem.at[2]),
        pltpu.make_async_copy(mix_hbm, mix_v, in_sem.at[3]),
    ]
    for load in loads:
        load.start()

    lon_down, lon_up = (lon + nlon - 1) % nlon, (lon + 1) % nlon
    has_above, has_below = lat > 0, lat < nlat - 1

    barrier = pltpu.get_barrier_semaphore()

    def greet(lon_to, lat_to):
        pl.semaphore_signal(
            barrier, inc=1, device_id={"lon": lon_to, "lat": lat_to}, device_id_type=MESH
        )

    greet(lon_down, lat)
    greet(lon_up, lat)
    extra = 0
    for axis, step in first:
        if axis == "lat":
            greet(lon, flip(lat, step))
        elif step > 1:
            greet(flip(lon, step), lat)
        extra += axis == "lat" or step > 1

    @pl.when(has_above)
    def _():
        for lon_to in (lon_down, lon, lon_up):
            greet(lon_to, lat - 1)

    @pl.when(has_below)
    def _():
        for lon_to in (lon_down, lon, lon_up):
            greet(lon_to, lat + 1)

    at0 = lax.broadcasted_iota(jnp.int32, (chans, chans), 0)
    at1 = lax.broadcasted_iota(jnp.int32, (chans, chans), 1)
    group = chans // rows
    eye = (at0 == at1).astype(BF16)
    gather = (at1 == (at0 % group) * rows + at0 // group).astype(BF16)
    scatter = (at0 == (at1 % group) * rows + at1 // group).astype(BF16)

    loads[0].wait()
    for b in range(rows):
        part = nn_dot(gather, cot_v[b * chans : (b + 1) * chans, :]).astype(BF16)
        for r in range(rows):
            by_row[r, b * group : (b + 1) * group, :] = part[r * group : (r + 1) * group]
    for r in range(rows):
        cot_t[r + 1, LON_REACH : LON_REACH + cols, :] = nt_dot(eye, by_row[r]).astype(BF16)

    loads[1].wait()

    @pl.when(jnp.logical_not(has_above))
    def _():
        cot_t[0] = jnp.zeros_like(cot_t[0])
        taps_v[2, 0] = jnp.zeros_like(taps_v[2, 0])

    @pl.when(jnp.logical_not(has_below))
    def _():
        cot_t[rows + 1] = jnp.zeros_like(cot_t[rows + 1])
        taps_v[0, rows + 1] = jnp.zeros_like(taps_v[0, rows + 1])

    pl.semaphore_wait(barrier, 2 + extra + 3 * has_above.astype(jnp.int32) + 3 * has_below.astype(jnp.int32))

    own = pl.ds(LON_REACH, cols)
    head, tail = pl.ds(LON_REACH, LON_REACH), pl.ds(cols, LON_REACH)
    left, right = pl.ds(0, LON_REACH), pl.ds(LON_REACH + cols, LON_REACH)
    every = pl.ds(1, rows)

    def halo(i, src, dst, lon_to, lat_to):
        return pltpu.make_async_remote_copy(
            src_ref=src, dst_ref=dst, send_sem=halo_send.at[i], recv_sem=halo_recv.at[i],
            device_id={"lon": lon_to, "lat": lat_to}, device_id_type=MESH,
        )

    sides = [
        halo(0, cot_t.at[every, head], cot_t.at[every, right], lon_down, lat),
        halo(1, cot_t.at[every, tail], cot_t.at[every, left], lon_up, lat),
    ]
    above, below = lat - 1, lat + 1
    upward = [
        halo(2, cot_t.at[1, own], cot_t.at[rows + 1, own], lon, above),
        halo(3, cot_t.at[1, head], cot_t.at[rows + 1, right], lon_down, above),
        halo(4, cot_t.at[1, tail], cot_t.at[rows + 1, left], lon_up, above),
        halo(5, taps_v.at[0, 1], taps_v.at[0, rows + 1], lon, above),
    ]
    downward = [
        halo(6, cot_t.at[rows, own], cot_t.at[0, own], lon, below),
        halo(7, cot_t.at[rows, head], cot_t.at[0, right], lon_down, below),
        halo(8, cot_t.at[rows, tail], cot_t.at[0, left], lon_up, below),
        halo(9, taps_v.at[2, rows], taps_v.at[2, 0], lon, below),
    ]

    @pl.when(has_above)
    def _():
        for copy in upward:
            copy.start()

    @pl.when(has_below)
    def _():
        for copy in downward:
            copy.start()

    for copy in sides:
        copy.start()

    loads[2].wait()
    for b in range(rows):
        part = nn_dot(gather, inp_v[b * chans : (b + 1) * chans, :]).astype(BF16)
        for r in range(rows):
            inp_r[b * group : (b + 1) * group, r * cols : (r + 1) * cols] = part[
                r * group : (r + 1) * group
            ]

    def widen(r):
        base = None
        for a in range(ROWS_A):
            row = taps_v[a, r + 2 - a].astype(F32)
            wide = jnp.concatenate([row, jnp.zeros_like(row)], axis=1)
            if a:
                wide = pltpu.roll(wide, a * WINDOW, 1)
            base = wide if base is None else base + wide
        for k in range(kernels):
            flat = jnp.broadcast_to(base[k : k + 1], (BLOCK, DEPTH))
            toep[r, k * BLOCK : (k + 1) * BLOCK, :] = pltpu.roll(
                flat, 0, 1, stride=1, stride_axis=0
            ).astype(BF16)

    def inner_rows(i, carry):
        widen(i)
        return carry

    lax.fori_loop(1, rows - 1, inner_rows, 0)

    for copy in sides:
        copy.wait()

    @pl.when(has_above)
    def _():
        for copy in upward:
            copy.wait_send()
        for copy in downward:
            copy.wait_recv()

    @pl.when(has_below)
    def _():
        for copy in downward:
            copy.wait_send()
        for copy in upward:
            copy.wait_recv()

    widen(0)
    widen(rows - 1)

    pad = jnp.zeros((DEPTH - ROWS_A * WINDOW, chans), BF16)
    full = cols // BLOCK
    rest = cols - full * BLOCK

    def spread_row(r, carry):
        base = pl.multiple_of(r * cols, cols)
        for jb in range(full + (rest > 0)):
            start = jb * BLOCK if jb < full else cols - BLOCK
            source = jnp.concatenate(
                [cot_t[r + 2 - a, start : start + WINDOW, :] for a in range(ROWS_A)] + [pad], axis=0
            )
            if jb < full:
                size, bands = BLOCK, toep[r]
            else:
                size = rest
                bands = jnp.concatenate(
                    [toep[r, (k + 1) * BLOCK - rest : (k + 1) * BLOCK, :] for k in range(kernels)], axis=0
                )
            out = nn_dot(bands, source).astype(BF16)
            for k in range(kernels):
                spread[pl.ds(base + jb * BLOCK, size), k * chans : (k + 1) * chans] = out[
                    k * size : (k + 1) * size
                ]
        return carry

    lax.fori_loop(0, rows, spread_row, 0)

    def partner(stage):
        (axis0, step0), (axis1, step1) = first[stage], second[stage]
        lon_to, lat_to, side = lon, lat, 0
        for mine, axis, step in ((1 - core, axis0, step0), (core, axis1, step1)):
            if axis == "lon":
                lon_to = lon_to + mine * (flip(lon, step) - lon)
                side = side + mine * ((lon // step) % 2)
            else:
                lat_to = lat_to + mine * (flip(lat, step) - lat)
                side = side + mine * ((lat // step) % 2)
        return lon_to, lat_to, side

    stages = len(first)
    partners = [partner(s) for s in range(stages)]
    sizes, offs = [], [0]
    n = chans
    for s in range(stages):
        halves = n >= 2 * TILE
        if halves:
            n //= 2
            offs.append(offs[-1] + partners[s][2] * n)
        sizes.append((n, halves))
    halving = sum(h for _, h in sizes)
    shard = n
    total_stages = 1 + stages + halving + 1

    def remote(g, slot, src, dst, lon_to, lat_to):
        return pltpu.make_async_remote_copy(
            src_ref=src, dst_ref=dst,
            send_sem=ar_send.at[g * total_stages + slot], recv_sem=ar_recv.at[g * total_stages + slot],
            device_id={"lon": lon_to, "lat": lat_to}, device_id_type=MESH,
        )

    def reduce_copy(g, s):
        ks = pl.ds(g * per, per)
        if s == 0:
            return remote(g, 0, snd0.at[ks], rcv0.at[ks], lon, flip(lat, 1))
        lon_to, lat_to, _ = partners[s - 1]
        return remote(g, s, snds[s - 1].at[ks], rcvs[s - 1].at[ks], lon_to, lat_to)

    def gather_copy(g, i):
        ks = pl.ds(g * per, per)
        if i == halving:
            block = gat.at[core, ks]
            return remote(g, 1 + stages + i, block, block, lon, flip(lat, 1))
        s = halving - 1 - i
        lon_to, lat_to, _ = partners[s]
        size = sizes[s][0]
        block = gat.at[core, ks, pl.ds(pl.multiple_of(offs[s + 1], TILE), size)]
        return remote(g, 1 + stages + i, block, block, lon_to, lat_to)

    def wg_part(g):
        for k in range(g * per, (g + 1) * per):
            part = nn_dot(inp_r[...], spread[:, k * chans : (k + 1) * chans])
            low, high = part[:, :LANES], part[:, LANES:]
            acc[k] = jnp.where(core == 0, low, high)
            snd0[k] = jnp.where(core == 0, high, low).astype(BF16)
        reduce_copy(g, 0).start()

    def reduce_step(g, s):
        reduce_copy(g, s - 1).wait()
        ks = slice(g * per, (g + 1) * per)
        prev_size = chans if s == 1 else sizes[s - 2][0]
        prev_halves = s == 1 or sizes[s - 2][1]
        own_ref = acc if s == 1 else accs[s - 2]
        got_ref = rcv0 if s == 1 else rcvs[s - 2]
        sent_ref = None if prev_halves else snds[s - 2]

        def total(start, size):
            at = pl.ds(start, size)
            mine = own_ref[ks, at] if prev_halves else sent_ref[ks, at].astype(F32)
            return mine + got_ref[ks, at].astype(F32)

        if s > stages:
            gat[core, ks, pl.ds(pl.multiple_of(offs[-1], TILE), shard)] = total(0, shard).astype(BF16)
            gather_copy(g, 0).start()
            return
        size, halves = sizes[s - 1]
        if halves:
            side = partners[s - 1][2]
            snds[s - 1][ks] = total(pl.multiple_of((1 - side) * size, TILE), size).astype(BF16)
            reduce_copy(g, s).start()
            accs[s - 1][ks] = total(pl.multiple_of(side * size, TILE), size)
        else:
            snds[s - 1][ks] = total(0, size).astype(BF16)
            reduce_copy(g, s).start()

    def wg_store(g):
        size = per * chans
        return pltpu.make_async_copy(
            wg_v.at[pl.ds(g * size, size)], wg_hbm.at[pl.ds(g * size, size)], out_sem.at[g]
        )

    def gather_step(g, i):
        gather_copy(g, i - 1).wait()
        if i <= halving:
            gather_copy(g, i).start()
            return
        for k in range(g * per, (g + 1) * per):
            for h in range(chans // LANES):
                start = k * chans + h * LANES
                wg_v[start : start + LANES, :] = nt_dot(eye[:LANES, :LANES], gat[h, k]).astype(BF16)
        wg_store(g).start()

    def ig_part(r):
        at = slice(r * cols, (r + 1) * cols)
        part = nn_dot(spread[at, :], mix_v[...]).astype(BF16)
        ig_row[r] = nt_dot(eye, part).astype(BF16)

    def ig_final(b):
        part = jnp.concatenate([ig_row[r, b * group : (b + 1) * group, :] for r in range(rows)], axis=0)
        ig_v[b * chans : (b + 1) * chans, :] = nn_dot(scatter, part).astype(BF16)

    ig_store = pltpu.make_async_copy(ig_v, ig_hbm, out_sem.at[GROUPS])

    def ig_end():
        ig_store.start()

    side_work = [functools.partial(ig_part, r) for r in range(rows)]
    side_work += [functools.partial(ig_final, b) for b in range(rows)] + [ig_end]

    steps = []
    for g in range(GROUPS):
        line = [functools.partial(wg_part, g)]
        line += [functools.partial(reduce_step, g, s) for s in range(1, stages + 2)]
        line += [functools.partial(gather_step, g, i) for i in range(1, halving + 2)]
        steps.append(line)

    loads[3].wait()
    for t in range(len(steps[0]) + GROUPS - 1):
        for g in range(GROUPS):
            if 0 <= t - g < len(steps[g]):
                steps[g][t - g]()
        if t >= GROUPS - 1:
            for _ in range(2):
                if side_work:
                    side_work.pop(0)()
    for work in side_work:
        work()
    for g in range(GROUPS):
        wg_store(g).wait()
    ig_store.wait()


def local(nlon, nlat, inputs, cotangent, mixing, filters, support):
    chans, rows, cols = inputs.shape
    kernels = filters.shape[0]
    offsets = jnp.arange(TAPS, dtype=jnp.int32) - LON_REACH
    keep = (jnp.abs(offsets)[None, :] <= support[:, None]).astype(BF16)
    coefs = filters * keep[None, :, None, :]
    taps = jnp.transpose(coefs[..., ::-1], (2, 1, 0, 3))
    taps = jnp.pad(taps, ((0, 0), (0, 0), (0, TILE - kernels), (0, LANES - TAPS)))

    first, _ = stage_orders(nlon, nlat)
    sizes, n = [], chans
    for _ in first:
        n = n // 2 if n >= 2 * TILE else n
        sizes.append(n)
    halving = sum(1 for i, s in enumerate(sizes) if s < ([chans] + sizes)[i])
    total_stages = 2 + len(first) + halving
    any_spec = pl.BlockSpec(memory_space=pl.ANY)
    vm = pltpu.VMEM
    flops = 2 * rows * cols * kernels * chans * chans * 3
    ig, wg = pl.pallas_call(
        functools.partial(kernel, nlon, nlat, kernels, chans, rows, cols),
        out_shape=(
            jax.ShapeDtypeStruct((chans * rows, cols), BF16),
            jax.ShapeDtypeStruct((kernels * chans, chans), BF16),
        ),
        in_specs=[any_spec] * 4,
        out_specs=(any_spec, any_spec),
        scratch_shapes=[
            vm((chans * rows, cols), BF16),
            vm((chans * rows, cols), BF16),
            vm((kernels * chans, chans), BF16),
            vm((ROWS_A, rows + 2, TILE, LANES), BF16),
            vm((rows, chans, cols), BF16),
            vm((chans, rows * cols), BF16),
            vm((rows + 2, cols + 2 * LON_REACH, chans), BF16),
            vm((rows, kernels * BLOCK, DEPTH), BF16),
            vm((rows * cols, kernels * chans), BF16),
            vm((kernels, chans, LANES), F32),
            vm((kernels, chans, LANES), BF16),
            vm((kernels, chans, LANES), BF16),
            [vm((kernels, s, LANES), F32) for s in sizes],
            [vm((kernels, s, LANES), BF16) for s in sizes],
            [vm((kernels, s, LANES), BF16) for s in sizes],
            vm((2, kernels, chans, LANES), BF16),
            vm((kernels * chans, chans), BF16),
            vm((rows, chans, cols), BF16),
            vm((chans * rows, cols), BF16),
            pltpu.SemaphoreType.DMA((4,)),
            pltpu.SemaphoreType.DMA((GROUPS + 1,)),
            pltpu.SemaphoreType.DMA((10,)),
            pltpu.SemaphoreType.DMA((10,)),
            pltpu.SemaphoreType.DMA((GROUPS * total_stages,)),
            pltpu.SemaphoreType.DMA((GROUPS * total_stages,)),
        ],
        compiler_params=pltpu.CompilerParams(
            collective_id=0, has_side_effects=True, vmem_limit_bytes=56 * 2**20
        ),
        cost_estimate=pl.CostEstimate(flops=flops, bytes_accessed=7 * 2**20, transcendentals=0),
    )(
        cotangent.reshape(chans * rows, cols),
        inputs.reshape(chans * rows, cols),
        mixing.reshape(kernels * chans, chans),
        taps,
    )
    scale = 1.0 / math.sqrt(rows * nlat * cols * nlon)
    weight_grad = wg.reshape(kernels, chans, chans).astype(F32) * scale
    return ig.reshape(chans, rows, cols), weight_grad


def solution(mesh):
    return jax.shard_map(
        functools.partial(local, mesh.shape["lon"], mesh.shape["lat"]),
        mesh=mesh,
        in_specs=(
            P(None, "lat", "lon"),
            P(None, "lat", "lon"),
            P(),
            P(None, "lat", None, None),
            P("lat"),
        ),
        out_specs=(P(None, "lat", "lon"), P()),
        check_vma=False,
    )
```

```python
import functools
import math

import jax
import jax.numpy as jnp
from jax import lax
from jax.experimental import pallas as pl
from jax.experimental.pallas import tpu as pltpu
from jax.sharding import PartitionSpec as P

LAT_REACH = 1
LON_REACH = 16
TAPS = 2 * LON_REACH + 1
ROWS_A = 2 * LAT_REACH + 1
BLOCK = 48
WINDOW = BLOCK + 2 * LON_REACH
DEPTH = 256
TILE = 16
LANES = 128
GROUPS = 3
QUARTER = 4

F32 = jnp.float32
BF16 = jnp.bfloat16
MESH = pl.DeviceIdType.MESH


def nt_dot(a, b):
    return lax.dot_general(a, b, (((1,), (1,)), ((), ())), preferred_element_type=F32)


def nn_dot(a, b):
    return lax.dot_general(a, b, (((1,), (0,)), ((), ())), preferred_element_type=F32)


def flip(index, step):
    return index + step - 2 * step * ((index // step) % 2)


def layout(nlon, nlat):
    copies = (nlon // (2 * QUARTER)) * (nlat // QUARTER)
    return QUARTER, QUARTER, copies


def kernel(
    nlon, nlat, kernels, chans, rows, cols,
    cot_hbm, inp_hbm, mix_hbm, filt_hbm, support, ig_hbm, wg_hbm,
    cot_v, inp_v, mix_v, filt_v, taps_v, taps_x, by_row, inp_r, cot_t, toep, spread,
    acc, snd0, rcv0, snd_a, acc_a, rcv_a, snd_b, acc_b, rcv_b, rcv_c, gat, ig_row, ig_v,
    in_sem, out_sem, halo_send, halo_recv, ar_send, ar_recv,
):
    lon, lat = lax.axis_index("lon"), lax.axis_index("lat")
    core = lat % 2
    per = kernels // GROUPS
    plane, line, copies = layout(nlon, nlat)

    loads = [
        pltpu.make_async_copy(cot_hbm, cot_v, in_sem.at[0]),
        pltpu.make_async_copy(filt_hbm, filt_v, in_sem.at[1]),
        pltpu.make_async_copy(inp_hbm, inp_v, in_sem.at[2]),
        pltpu.make_async_copy(mix_hbm, mix_v, in_sem.at[3]),
    ]
    for load in loads:
        load.start()

    lon_down, lon_up = (lon + nlon - 1) % nlon, (lon + 1) % nlon
    has_above, has_below = lat > 0, lat < nlat - 1

    x, y = lon % 2, (lat // 2) % 2
    z = (lon // 2) % line
    beyond = (lon // (2 * line)) * (nlat // 4) + lat // 4

    def plane_to(d):
        return (flip(lon, 1) if d % 2 else lon), (flip(lat, 2) if d // 2 else lat)

    def line_to(d):
        return lon + 2 * ((z + d) % line - z), lat

    def copy_to(d):
        to = (beyond + d) % copies
        lon_to = (to // (nlat // 4)) * (2 * line) + lon % (2 * line)
        return lon_to, (to % (nlat // 4)) * 4 + lat % 4

    barrier = pltpu.get_barrier_semaphore()

    def greet(lon_to, lat_to):
        pl.semaphore_signal(
            barrier, inc=1, device_id={"lon": lon_to, "lat": lat_to}, device_id_type=MESH
        )

    partners = [plane_to(d) for d in range(1, plane)] + [line_to(d) for d in range(1, line)]
    partners += [copy_to(d) for d in range(1, copies)]

    @pl.when(has_above)
    def _():
        for lon_to in (lon_down, lon, lon_up):
            greet(lon_to, lat - 1)

    @pl.when(has_below)
    def _():
        for lon_to in (lon_down, lon, lon_up):
            greet(lon_to, lat + 1)

    greet(lon_down, lat)
    greet(lon_up, lat)
    for lon_to, lat_to in partners:
        greet(lon_to, lat_to)

    at0 = lax.broadcasted_iota(jnp.int32, (chans, chans), 0)
    at1 = lax.broadcasted_iota(jnp.int32, (chans, chans), 1)
    group = chans // rows
    eye = (at0 == at1).astype(BF16)
    gather = (at1 == (at0 % group) * rows + at0 // group).astype(BF16)
    scatter = (at0 == (at1 % group) * rows + at1 // group).astype(BF16)

    loads[1].wait()
    filt_rows = kernels * ROWS_A * rows
    lane = lax.broadcasted_iota(jnp.int32, (rows, TAPS), 1)
    sub = lax.broadcasted_iota(jnp.int32, (rows, TAPS), 0)
    reach = jnp.zeros((rows, TAPS), jnp.int32)
    for r in range(rows):
        reach = jnp.where(sub == r, support[r], reach)
    keep = (jnp.abs(lane - LON_REACH) <= reach).astype(F32)
    coefs = filt_v[...].astype(F32).reshape(kernels * ROWS_A, rows, TAPS) * keep[None]
    coefs = coefs.reshape(filt_rows, TAPS).astype(BF16)
    out_rows = (rows + 2) * TILE
    pick0 = lax.broadcasted_iota(jnp.int32, (out_rows, filt_rows), 0)
    pick1 = lax.broadcasted_iota(jnp.int32, (out_rows, filt_rows), 1)
    tap = lax.broadcasted_iota(jnp.int32, (TAPS, DEPTH), 0)
    spot = lax.broadcasted_iota(jnp.int32, (TAPS, DEPTH), 1)
    placed = jnp.zeros((out_rows, DEPTH), F32)
    for a in range(ROWS_A):
        row = pick0 // TILE - a
        k = pick0 % TILE
        pick = (pick1 == k * (ROWS_A * rows) + a * rows + row) & (row >= 0) & (row < rows) & (k < kernels)
        chosen = nn_dot(pick.astype(BF16), coefs).astype(BF16)
        placed += nn_dot(chosen, (spot == a * WINDOW + TAPS - 1 - tap).astype(BF16))
    taps_v[...] = placed.astype(BF16).reshape(rows + 2, TILE, DEPTH)

    @pl.when(jnp.logical_not(has_above))
    def _():
        cot_t[0] = jnp.zeros_like(cot_t[0])
        taps_x[0] = jnp.zeros_like(taps_x[0])

    @pl.when(jnp.logical_not(has_below))
    def _():
        cot_t[rows + 1] = jnp.zeros_like(cot_t[rows + 1])
        taps_x[1] = jnp.zeros_like(taps_x[1])

    loads[0].wait()
    for b in range(rows):
        part = nn_dot(gather, cot_v[b * chans : (b + 1) * chans, :]).astype(BF16)
        for r in range(rows):
            by_row[r, b * group : (b + 1) * group, :] = part[r * group : (r + 1) * group]
    for r in range(rows):
        cot_t[r + 1, LON_REACH : LON_REACH + cols, :] = nt_dot(eye, by_row[r]).astype(BF16)

    edges = has_above.astype(jnp.int32) + has_below.astype(jnp.int32)
    pl.semaphore_wait(barrier, 2 + len(partners) + 3 * edges)

    own = pl.ds(LON_REACH, cols)
    head, tail = pl.ds(LON_REACH, LON_REACH), pl.ds(cols, LON_REACH)
    left, right = pl.ds(0, LON_REACH), pl.ds(LON_REACH + cols, LON_REACH)
    every = pl.ds(1, rows)

    def halo(i, src, dst, lon_to, lat_to):
        return pltpu.make_async_remote_copy(
            src_ref=src, dst_ref=dst, send_sem=halo_send.at[i], recv_sem=halo_recv.at[i],
            device_id={"lon": lon_to, "lat": lat_to}, device_id_type=MESH,
        )

    sides = [
        halo(0, cot_t.at[every, head], cot_t.at[every, right], lon_down, lat),
        halo(1, cot_t.at[every, tail], cot_t.at[every, left], lon_up, lat),
    ]
    above, below = lat - 1, lat + 1
    upward = [
        halo(2, cot_t.at[1, own], cot_t.at[rows + 1, own], lon, above),
        halo(3, cot_t.at[1, head], cot_t.at[rows + 1, right], lon_down, above),
        halo(4, cot_t.at[1, tail], cot_t.at[rows + 1, left], lon_up, above),
        halo(5, taps_v.at[0], taps_x.at[1], lon, above),
    ]
    downward = [
        halo(6, cot_t.at[rows, own], cot_t.at[0, own], lon, below),
        halo(7, cot_t.at[rows, head], cot_t.at[0, right], lon_down, below),
        halo(8, cot_t.at[rows, tail], cot_t.at[0, left], lon_up, below),
        halo(9, taps_v.at[rows + 1], taps_x.at[0], lon, below),
    ]

    for copy in sides:
        copy.start()

    @pl.when(has_above)
    def _():
        for copy in upward:
            copy.start()

    @pl.when(has_below)
    def _():
        for copy in downward:
            copy.start()

    def widen(r, more=None):
        base = taps_v[r + 1].astype(F32)
        if more is not None:
            base += taps_x[more].astype(F32)
        for k in range(kernels):
            flat = jnp.broadcast_to(base[k : k + 1], (BLOCK, DEPTH))
            toep[r, k * BLOCK : (k + 1) * BLOCK, :] = pltpu.roll(
                flat, 0, 1, stride=1, stride_axis=0
            ).astype(BF16)

    pad = jnp.zeros((DEPTH - ROWS_A * WINDOW, chans), BF16)
    full = cols // BLOCK
    rest = cols - full * BLOCK
    blocks = full + (rest > 0)
    inside = [jb for jb in range(full) if jb > 0 and (jb + 1) * BLOCK + LON_REACH <= cols]

    def spread_blocks(r, which):
        base = pl.multiple_of(r * cols, cols)
        for jb in which:
            start = jb * BLOCK if jb < full else cols - BLOCK
            source = jnp.concatenate(
                [cot_t[r + 2 - a, start : start + WINDOW, :] for a in range(ROWS_A)] + [pad], axis=0
            )
            if jb < full:
                size, bands = BLOCK, toep[r]
            else:
                size = rest
                bands = jnp.concatenate(
                    [toep[r, (k + 1) * BLOCK - rest : (k + 1) * BLOCK, :] for k in range(kernels)], axis=0
                )
            out = nn_dot(bands, source).astype(BF16)
            for k in range(kernels):
                spread[pl.ds(base + jb * BLOCK, size), k * chans : (k + 1) * chans] = out[
                    k * size : (k + 1) * size
                ]

    def inner_row(r, carry):
        widen(r)
        spread_blocks(r, inside)
        return carry

    lax.fori_loop(1, rows - 1, inner_row, 0)

    loads[2].wait()
    for b in range(rows):
        part = nn_dot(gather, inp_v[b * chans : (b + 1) * chans, :]).astype(BF16)
        for r in range(rows):
            inp_r[b * group : (b + 1) * group, r * cols : (r + 1) * cols] = part[
                r * group : (r + 1) * group
            ]

    for copy in sides:
        copy.wait()

    def side_row(r, carry):
        spread_blocks(r, [jb for jb in range(blocks) if jb not in inside])
        return carry

    lax.fori_loop(1, rows - 1, side_row, 0)

    @pl.when(has_above)
    def _():
        for copy in upward:
            copy.wait_send()
        for copy in downward:
            copy.wait_recv()

    @pl.when(has_below)
    def _():
        for copy in downward:
            copy.wait_send()
        for copy in upward:
            copy.wait_recv()

    widen(0, 0)
    widen(rows - 1, 1)

    def end_row(i, carry):
        spread_blocks(i * (rows - 1), range(blocks))
        return carry

    lax.fori_loop(0, 2, end_row, 0)

    quarter, shard = chans // plane, chans // (plane * line)
    mine_a = x * 2 + y
    first_a = pl.multiple_of(mine_a * quarter, quarter)
    first_b = pl.multiple_of(mine_a * quarter + z * shard, shard)
    n_a, n_b, n_c = plane - 1, line - 1, copies - 1
    slots = 2 + 2 * n_a + 2 * n_b + n_c

    def remote(g, slot, src, dst, to):
        at = g * slots + slot
        return pltpu.make_async_remote_copy(
            src_ref=src, dst_ref=dst, send_sem=ar_send.at[at], recv_sem=ar_recv.at[at],
            device_id={"lon": to[0], "lat": to[1]}, device_id_type=MESH,
        )

    def core_copies(g):
        ks = pl.ds(g * per, per)
        return [remote(g, 0, snd0.at[ks], rcv0.at[ks], (lon, flip(lat, 1)))]

    def plane_copies(g):
        ks, out = pl.ds(g * per, per), []
        for d in range(1, plane):
            x_to = flip(x, 1) if d % 2 else x
            y_to = flip(y, 1) if d // 2 else y
            start = pl.multiple_of((x_to * 2 + y_to) * quarter, quarter)
            out.append(
                remote(g, d, snd_a.at[ks, pl.ds(start, quarter)], rcv_a.at[d - 1, ks], plane_to(d))
            )
        return out

    def line_copies(g):
        ks, out = pl.ds(g * per, per), []
        for d in range(1, line):
            start = pl.multiple_of(((z + d) % line) * shard, shard)
            out.append(
                remote(g, n_a + d, snd_b.at[ks, pl.ds(start, shard)], rcv_b.at[d - 1, ks], line_to(d))
            )
        return out

    def beyond_copies(g):
        ks = pl.ds(g * per, per)
        return [
            remote(g, n_a + n_b + d, rcv_c.at[beyond, ks], rcv_c.at[beyond, ks], copy_to(d))
            for d in range(1, copies)
        ]

    def gather_copies(g, count, base, start, size, to):
        block = gat.at[core, pl.ds(g * per, per), pl.ds(start, size)]
        return [remote(g, base + d, block, block, to(d)) for d in range(1, count)]

    def line_gather(g):
        return gather_copies(g, line, n_a + n_b + n_c, first_b, shard, line_to)

    def plane_gather(g):
        return gather_copies(g, plane, n_a + 2 * n_b + n_c, first_a, quarter, plane_to)

    def core_gather(g):
        block = gat.at[core, pl.ds(g * per, per)]
        return [remote(g, slots - 1, block, block, (lon, flip(lat, 1)))]

    def start(copies_of):
        for copy in copies_of:
            copy.start()

    def wait(copies_of):
        for copy in copies_of:
            copy.wait()

    def product(g):
        for k in range(g * per, (g + 1) * per):
            part = nn_dot(inp_r[...], spread[:, k * chans : (k + 1) * chans])
            low, high = part[:, :LANES], part[:, LANES:]
            acc[k] = jnp.where(core == 0, low, high)
            snd0[k] = jnp.where(core == 0, high, low).astype(BF16)
        start(core_copies(g))

    def core_sum(g):
        wait(core_copies(g))
        ks = slice(g * per, (g + 1) * per)
        snd_a[ks] = (acc[ks] + rcv0[ks].astype(F32)).astype(BF16)
        start(plane_copies(g))
        at = pl.ds(first_a, quarter)
        acc_a[ks] = acc[ks, at] + rcv0[ks, at].astype(F32)

    def plane_sum(g):
        wait(plane_copies(g))
        ks = slice(g * per, (g + 1) * per)
        total = acc_a[ks]
        for d in range(n_a):
            total += rcv_a[d, ks].astype(F32)
        acc_b[ks] = total
        snd_b[ks] = total.astype(BF16)
        start(line_copies(g))

    def line_sum(g):
        wait(line_copies(g))
        ks = slice(g * per, (g + 1) * per)
        total = acc_b[ks, pl.ds(pl.multiple_of(z * shard, shard), shard)]
        for d in range(n_b):
            total += rcv_b[d, ks].astype(F32)
        if copies > 1:
            rcv_c[beyond, ks] = total.astype(BF16)
            start(beyond_copies(g))
            wait(beyond_copies(g))
            total = rcv_c[0, ks].astype(F32)
            for d in range(1, copies):
                total += rcv_c[d, ks].astype(F32)
        gat[core, ks, pl.ds(first_b, shard)] = total.astype(BF16)
        start(line_gather(g))

    def line_done(g):
        wait(line_gather(g))
        start(plane_gather(g))

    def plane_done(g):
        wait(plane_gather(g))
        start(core_gather(g))

    def wg_store(g):
        ks = pl.ds(g * per, per)
        return pltpu.make_async_copy(gat.at[:, ks], wg_hbm.at[:, ks], out_sem.at[g])

    def core_done(g):
        wait(core_gather(g))
        wg_store(g).start()

    def ig_part(r):
        at = slice(r * cols, (r + 1) * cols)
        part = nn_dot(spread[at, :], mix_v[...]).astype(BF16)
        ig_row[r] = nt_dot(eye, part).astype(BF16)

    def ig_final(b):
        part = jnp.concatenate([ig_row[r, b * group : (b + 1) * group, :] for r in range(rows)], axis=0)
        ig_v[b * chans : (b + 1) * chans, :] = nn_dot(scatter, part).astype(BF16)

    ig_store = pltpu.make_async_copy(ig_v, ig_hbm, out_sem.at[GROUPS])

    side_work = [functools.partial(ig_part, r) for r in range(rows)]
    side_work += [functools.partial(ig_final, b) for b in range(rows)] + [ig_store.start]

    steps = []
    for g in range(GROUPS):
        for s, step in enumerate((core_sum, plane_sum, line_sum, line_done, plane_done, core_done)):
            steps.append((2 * s + g, s, functools.partial(step, g)))
    steps = [step for _, _, step in sorted(steps, key=lambda item: item[:2])]

    loads[3].wait()
    product(0)
    for g in range(1, GROUPS):
        product(g)
        steps.pop(0)() if g == 1 else None
    for i, step in enumerate(steps):
        if side_work:
            side_work.pop(0)()
        step()
    for work in side_work:
        work()
    for g in range(GROUPS):
        wg_store(g).wait()
    ig_store.wait()


def finish(scale, gat_hbm, ig_hbm, wg_hbm, out_hbm, gat_v, wg_v, ig_v, in_sem, wg_sem, ig_sem):
    _, kernels, chans, _ = gat_v.shape
    fetches = [
        pltpu.make_async_copy(gat_hbm.at[:, k], gat_v.at[:, k], in_sem.at[k]) for k in range(kernels)
    ]
    for fetch in fetches:
        fetch.start()
    ig_in = pltpu.make_async_copy(ig_hbm, ig_v, ig_sem.at[0])
    ig_out = pltpu.make_async_copy(ig_v, out_hbm, ig_sem.at[1])
    ig_in.start()
    at0 = lax.broadcasted_iota(jnp.int32, (LANES, LANES), 0)
    at1 = lax.broadcasted_iota(jnp.int32, (LANES, LANES), 1)
    eye = (at0 == at1).astype(BF16)
    stores = []
    for k in range(kernels):
        fetches[k].wait()
        for h in range(chans // LANES):
            start = k * chans + h * LANES
            wg_v[start : start + LANES, :] = nt_dot(eye, gat_v[h, k]) * scale
        rows = pl.ds(k * chans, chans)
        stores.append(pltpu.make_async_copy(wg_v.at[rows], wg_hbm.at[rows], wg_sem.at[k]))
        stores[-1].start()
        if k == kernels // 2:
            ig_in.wait()
            ig_out.start()
    for store in stores:
        store.wait()
    ig_out.wait()


def local(nlon, nlat, inputs, cotangent, mixing, filters, support):
    chans, rows, cols = inputs.shape
    kernels = filters.shape[0]
    plane, line, copies = layout(nlon, nlat)
    quarter, shard = chans // plane, chans // (plane * line)
    slots = GROUPS * (2 + 2 * (plane - 1) + 2 * (line - 1) + copies - 1)
    any_spec = pl.BlockSpec(memory_space=pl.ANY)
    vm = pltpu.VMEM
    flops = 2 * rows * cols * kernels * chans * chans * 3
    ig, wg = pl.pallas_call(
        functools.partial(kernel, nlon, nlat, kernels, chans, rows, cols),
        out_shape=(
            jax.ShapeDtypeStruct((chans * rows, cols), BF16),
            jax.ShapeDtypeStruct((2, kernels, chans, LANES), BF16),
        ),
        in_specs=[any_spec] * 4 + [pl.BlockSpec(memory_space=pltpu.SMEM)],
        out_specs=(any_spec, any_spec),
        scratch_shapes=[
            vm((chans * rows, cols), BF16),
            vm((chans * rows, cols), BF16),
            vm((kernels * chans, chans), BF16),
            vm((kernels * ROWS_A * rows, TAPS), BF16),
            vm((rows + 2, TILE, DEPTH), BF16),
            vm((2, TILE, DEPTH), BF16),
            vm((rows, chans, cols), BF16),
            vm((chans, rows * cols), BF16),
            vm((rows + 2, cols + 2 * LON_REACH, chans), BF16),
            vm((rows, kernels * BLOCK, DEPTH), BF16),
            vm((rows * cols, kernels * chans), BF16),
            vm((kernels, chans, LANES), F32),
            vm((kernels, chans, LANES), BF16),
            vm((kernels, chans, LANES), BF16),
            vm((kernels, chans, LANES), BF16),
            vm((kernels, quarter, LANES), F32),
            vm((plane - 1, kernels, quarter, LANES), BF16),
            vm((kernels, quarter, LANES), BF16),
            vm((kernels, quarter, LANES), F32),
            vm((line - 1, kernels, shard, LANES), BF16),
            vm((copies, kernels, shard, LANES), BF16),
            vm((2, kernels, chans, LANES), BF16),
            vm((rows, chans, cols), BF16),
            vm((chans * rows, cols), BF16),
            pltpu.SemaphoreType.DMA((4,)),
            pltpu.SemaphoreType.DMA((GROUPS + 1,)),
            pltpu.SemaphoreType.DMA((10,)),
            pltpu.SemaphoreType.DMA((10,)),
            pltpu.SemaphoreType.DMA((slots,)),
            pltpu.SemaphoreType.DMA((slots,)),
        ],
        compiler_params=pltpu.CompilerParams(
            collective_id=0, has_side_effects=True, vmem_limit_bytes=56 * 2**20
        ),
        cost_estimate=pl.CostEstimate(flops=flops, bytes_accessed=7 * 2**20, transcendentals=0),
    )(
        cotangent.reshape(chans * rows, cols),
        inputs.reshape(chans * rows, cols),
        mixing.reshape(kernels * chans, chans),
        jnp.transpose(filters, (0, 2, 1, 3)).reshape(kernels * ROWS_A * rows, TAPS),
        support,
    )
    scale = 1.0 / math.sqrt(rows * nlat * cols * nlon)
    weight_grad, input_grad = pl.pallas_call(
        functools.partial(finish, scale),
        out_shape=(
            jax.ShapeDtypeStruct((kernels * chans, chans), F32),
            jax.ShapeDtypeStruct((chans * rows, cols), BF16),
        ),
        in_specs=[any_spec] * 2,
        out_specs=(any_spec, any_spec),
        scratch_shapes=[
            vm((2, kernels, chans, LANES), BF16),
            vm((kernels * chans, chans), F32),
            vm((chans * rows, cols), BF16),
            pltpu.SemaphoreType.DMA((kernels,)),
            pltpu.SemaphoreType.DMA((kernels,)),
            pltpu.SemaphoreType.DMA((2,)),
        ],
        compiler_params=pltpu.CompilerParams(vmem_limit_bytes=56 * 2**20),
    )(wg, ig)
    return input_grad.reshape(chans, rows, cols), weight_grad.reshape(kernels, chans, chans)


def solution(mesh):
    return jax.shard_map(
        functools.partial(local, mesh.shape["lon"], mesh.shape["lat"]),
        mesh=mesh,
        in_specs=(
            P(None, "lat", "lon"),
            P(None, "lat", "lon"),
            P(),
            P(None, "lat", None, None),
            P("lat"),
        ),
        out_specs=(P(None, "lat", "lon"), P()),
        check_vma=False,
    )
```

```python
import functools
import math

import jax
import jax.numpy as jnp
from jax import lax
from jax.experimental import pallas as pl
from jax.experimental.pallas import tpu as pltpu
from jax.sharding import PartitionSpec as P

LAT_REACH = 1
LON_REACH = 16
TAPS = 2 * LON_REACH + 1
ROWS_A = 2 * LAT_REACH + 1
BLOCK = 48
WINDOW = BLOCK + 2 * LON_REACH
DEPTH = 256
TILE = 16
LANES = 128
QUARTER = 4
PARTS = ((0, 4, "plane"), (4, 3, "plane"), (7, 2, "line"))
GROUPS = len(PARTS)
PACE = 2

F32 = jnp.float32
BF16 = jnp.bfloat16
MESH = pl.DeviceIdType.MESH


def nt_dot(a, b):
    return lax.dot_general(a, b, (((1,), (1,)), ((), ())), preferred_element_type=F32)


def nn_dot(a, b):
    return lax.dot_general(a, b, (((1,), (0,)), ((), ())), preferred_element_type=F32)


def flip(index, step):
    return index + step - 2 * step * ((index // step) % 2)


def layout(nlon, nlat):
    copies = (nlon // (2 * QUARTER)) * (nlat // QUARTER)
    return QUARTER, QUARTER, copies


def kernel(
    nlon, nlat, kernels, chans, rows, cols,
    cot_hbm, inp_hbm, mix_hbm, filt_hbm, support_hbm, ig_hbm, wg_hbm,
    cot_v, inp_v, mix_v, filt_v, support, taps_v, taps_x, by_row, inp_r, cot_t, toep, spread,
    acc, snd0, rcv0, snd_a, acc_a, rcv_a, snd_b, acc_b, rcv_b, rcv_c, gat, ig_row, ig_v,
    in_sem, out_sem, halo_send, halo_recv, ar_send, ar_recv,
):
    lon, lat = lax.axis_index("lon"), lax.axis_index("lat")
    core = lat % 2
    plane, line, copies = layout(nlon, nlat)

    loads = [
        pltpu.make_async_copy(cot_hbm, cot_v, in_sem.at[0]),
        pltpu.make_async_copy(filt_hbm, filt_v, in_sem.at[1]),
        pltpu.make_async_copy(inp_hbm, inp_v, in_sem.at[2]),
        pltpu.make_async_copy(mix_hbm, mix_v, in_sem.at[3]),
        pltpu.make_async_copy(support_hbm, support, in_sem.at[4]),
    ]
    for load in loads:
        load.start()

    lon_down, lon_up = (lon + nlon - 1) % nlon, (lon + 1) % nlon
    has_above, has_below = lat > 0, lat < nlat - 1

    x, y = lon % 2, (lat // 2) % 2
    z = (lon // 2) % line
    beyond = (lon // (2 * line)) * (nlat // 4) + lat // 4

    def plane_to(d):
        return (flip(lon, 1) if d % 2 else lon), (flip(lat, 2) if d // 2 else lat)

    def line_to(d):
        return lon + 2 * ((z + d) % line - z), lat

    def copy_to(d):
        to = (beyond + d) % copies
        lon_to = (to // (nlat // 4)) * (2 * line) + lon % (2 * line)
        return lon_to, (to % (nlat // 4)) * 4 + lat % 4

    barrier = pltpu.get_barrier_semaphore()

    def greet(lon_to, lat_to):
        pl.semaphore_signal(
            barrier, inc=1, device_id={"lon": lon_to, "lat": lat_to}, device_id_type=MESH
        )

    partners = [plane_to(d) for d in range(1, plane)] + [line_to(d) for d in range(1, line)]
    partners += [copy_to(d) for d in range(1, copies)]

    @pl.when(has_above)
    def _():
        for lon_to in (lon_down, lon, lon_up):
            greet(lon_to, lat - 1)

    @pl.when(has_below)
    def _():
        for lon_to in (lon_down, lon, lon_up):
            greet(lon_to, lat + 1)

    greet(lon_down, lat)
    greet(lon_up, lat)
    for lon_to, lat_to in partners:
        greet(lon_to, lat_to)

    at0 = lax.broadcasted_iota(jnp.int32, (chans, chans), 0)
    at1 = lax.broadcasted_iota(jnp.int32, (chans, chans), 1)
    group = chans // rows
    eye = (at0 == at1).astype(BF16)
    gather = (at1 == (at0 % group) * rows + at0 // group).astype(BF16)
    scatter = (at0 == (at1 % group) * rows + at1 // group).astype(BF16)

    loads[1].wait()
    loads[4].wait()
    filt_rows = kernels * ROWS_A * rows
    lane = lax.broadcasted_iota(jnp.int32, (rows, TAPS), 1)
    sub = lax.broadcasted_iota(jnp.int32, (rows, TAPS), 0)
    reach = jnp.zeros((rows, TAPS), jnp.int32)
    for r in range(rows):
        reach = jnp.where(sub == r, support[r], reach)
    keep = (jnp.abs(lane - LON_REACH) <= reach).astype(F32)
    coefs = filt_v[...].astype(F32).reshape(kernels * ROWS_A, rows, TAPS) * keep[None]
    coefs = coefs.reshape(filt_rows, TAPS).astype(BF16)
    out_rows = (rows + 2) * TILE
    pick0 = lax.broadcasted_iota(jnp.int32, (out_rows, filt_rows), 0)
    pick1 = lax.broadcasted_iota(jnp.int32, (out_rows, filt_rows), 1)
    tap = lax.broadcasted_iota(jnp.int32, (TAPS, DEPTH), 0)
    spot = lax.broadcasted_iota(jnp.int32, (TAPS, DEPTH), 1)
    placed = jnp.zeros((out_rows, DEPTH), F32)
    for a in range(ROWS_A):
        row = pick0 // TILE - a
        k = pick0 % TILE
        pick = (pick1 == k * (ROWS_A * rows) + a * rows + row) & (row >= 0) & (row < rows) & (k < kernels)
        chosen = nn_dot(pick.astype(BF16), coefs).astype(BF16)
        placed += nn_dot(chosen, (spot == a * WINDOW + TAPS - 1 - tap).astype(BF16))
    taps_v[...] = placed.astype(BF16).reshape(rows + 2, TILE, DEPTH)

    @pl.when(jnp.logical_not(has_above))
    def _():
        cot_t[0] = jnp.zeros_like(cot_t[0])
        taps_x[0] = jnp.zeros_like(taps_x[0])

    @pl.when(jnp.logical_not(has_below))
    def _():
        cot_t[rows + 1] = jnp.zeros_like(cot_t[rows + 1])
        taps_x[1] = jnp.zeros_like(taps_x[1])

    loads[0].wait()
    for b in range(rows):
        part = nn_dot(gather, cot_v[b * chans : (b + 1) * chans, :]).astype(BF16)
        for r in range(rows):
            by_row[r, b * group : (b + 1) * group, :] = part[r * group : (r + 1) * group]
    for r in range(rows):
        cot_t[r + 1, LON_REACH : LON_REACH + cols, :] = nt_dot(eye, by_row[r]).astype(BF16)

    edges = has_above.astype(jnp.int32) + has_below.astype(jnp.int32)
    pl.semaphore_wait(barrier, 2 + len(partners) + 3 * edges)

    own = pl.ds(LON_REACH, cols)
    head, tail = pl.ds(LON_REACH, LON_REACH), pl.ds(cols, LON_REACH)
    left, right = pl.ds(0, LON_REACH), pl.ds(LON_REACH + cols, LON_REACH)
    every = pl.ds(1, rows)

    def halo(i, src, dst, lon_to, lat_to):
        return pltpu.make_async_remote_copy(
            src_ref=src, dst_ref=dst, send_sem=halo_send.at[i], recv_sem=halo_recv.at[i],
            device_id={"lon": lon_to, "lat": lat_to}, device_id_type=MESH,
        )

    sides = [
        halo(0, cot_t.at[every, head], cot_t.at[every, right], lon_down, lat),
        halo(1, cot_t.at[every, tail], cot_t.at[every, left], lon_up, lat),
    ]
    above, below = lat - 1, lat + 1
    upward = [
        halo(2, cot_t.at[1, own], cot_t.at[rows + 1, own], lon, above),
        halo(3, cot_t.at[1, head], cot_t.at[rows + 1, right], lon_down, above),
        halo(4, cot_t.at[1, tail], cot_t.at[rows + 1, left], lon_up, above),
        halo(5, taps_v.at[0], taps_x.at[1], lon, above),
    ]
    downward = [
        halo(6, cot_t.at[rows, own], cot_t.at[0, own], lon, below),
        halo(7, cot_t.at[rows, head], cot_t.at[0, right], lon_down, below),
        halo(8, cot_t.at[rows, tail], cot_t.at[0, left], lon_up, below),
        halo(9, taps_v.at[rows + 1], taps_x.at[0], lon, below),
    ]

    for copy in sides:
        copy.start()

    @pl.when(has_above)
    def _():
        for copy in upward:
            copy.start()

    @pl.when(has_below)
    def _():
        for copy in downward:
            copy.start()

    def widen(r, more=None):
        base = taps_v[r + 1].astype(F32)
        if more is not None:
            base += taps_x[more].astype(F32)
        for k in range(kernels):
            flat = jnp.broadcast_to(base[k : k + 1], (BLOCK, DEPTH))
            toep[r, k * BLOCK : (k + 1) * BLOCK, :] = pltpu.roll(
                flat, 0, 1, stride=1, stride_axis=0
            ).astype(BF16)

    pad = jnp.zeros((DEPTH - ROWS_A * WINDOW, chans), BF16)
    full = cols // BLOCK
    rest = cols - full * BLOCK
    blocks = full + (rest > 0)
    inside = [jb for jb in range(full) if jb > 0 and (jb + 1) * BLOCK + LON_REACH <= cols]

    def spread_blocks(r, which, k0=0, kn=kernels):
        base = pl.multiple_of(r * cols, cols)
        for jb in which:
            start = jb * BLOCK if jb < full else cols - BLOCK
            source = jnp.concatenate(
                [cot_t[r + 2 - a, start : start + WINDOW, :] for a in range(ROWS_A)] + [pad], axis=0
            )
            if jb < full:
                size, bands = BLOCK, toep[r, k0 * BLOCK : (k0 + kn) * BLOCK, :]
            else:
                size = rest
                bands = jnp.concatenate(
                    [toep[r, (k + 1) * BLOCK - rest : (k + 1) * BLOCK, :] for k in range(k0, k0 + kn)], axis=0
                )
            out = nn_dot(bands, source).astype(BF16)
            for k in range(kn):
                spread[pl.ds(base + jb * BLOCK, size), (k0 + k) * chans : (k0 + k + 1) * chans] = out[
                    k * size : (k + 1) * size
                ]

    def inner_row(r, carry):
        widen(r)
        spread_blocks(r, inside)
        return carry

    lax.fori_loop(1, rows - 1, inner_row, 0)

    loads[2].wait()
    for b in range(rows):
        part = nn_dot(gather, inp_v[b * chans : (b + 1) * chans, :]).astype(BF16)
        for r in range(rows):
            inp_r[b * group : (b + 1) * group, r * cols : (r + 1) * cols] = part[
                r * group : (r + 1) * group
            ]

    for copy in sides:
        copy.wait()

    @pl.when(has_above)
    def _():
        for copy in upward:
            copy.wait_send()
        for copy in downward:
            copy.wait_recv()

    @pl.when(has_below)
    def _():
        for copy in downward:
            copy.wait_send()
        for copy in upward:
            copy.wait_recv()

    widen(0, 0)
    widen(rows - 1, 1)

    def edge_blocks(k0, kn):
        def side_row(r, carry):
            spread_blocks(r, [jb for jb in range(blocks) if jb not in inside], k0, kn)
            return carry

        def end_row(i, carry):
            spread_blocks(i * (rows - 1), range(blocks), k0, kn)
            return carry

        lax.fori_loop(1, rows - 1, side_row, 0)
        lax.fori_loop(0, 2, end_row, 0)

    quarter, shard = chans // plane, chans // (plane * line)
    count = {"plane": plane, "line": line}
    mine = {"plane": x * 2 + y, "line": z}
    n_a, n_b, n_c = plane - 1, line - 1, copies - 1
    slots = 2 + 2 * n_a + 2 * n_b + n_c

    def member(kind, d):
        if kind == "line":
            return line_to(d), (z + d) % line
        x_to = flip(x, 1) if d % 2 else x
        y_to = flip(y, 1) if d // 2 else y
        return plane_to(d), x_to * 2 + y_to

    def order(g):
        k0, kn, one = PARTS[g]
        return k0, kn, one, ("line" if one == "plane" else "plane")

    def first_at(g):
        return pl.multiple_of(mine[order(g)[2]] * quarter, quarter)

    def second_at(g):
        return pl.multiple_of(mine[order(g)[2]] * quarter + mine[order(g)[3]] * shard, shard)

    def remote(g, slot, src, dst, to):
        at = g * slots + slot
        return pltpu.make_async_remote_copy(
            src_ref=src, dst_ref=dst, send_sem=ar_send.at[at], recv_sem=ar_recv.at[at],
            device_id={"lon": to[0], "lat": to[1]}, device_id_type=MESH,
        )

    def core_copies(g):
        ks = pl.ds(*PARTS[g][:2])
        return [remote(g, 0, snd0.at[ks], rcv0.at[ks], (lon, flip(lat, 1)))]

    def split_copies(g, kind, base, size, src, dst):
        ks, out = pl.ds(*PARTS[g][:2]), []
        for d in range(1, count[kind]):
            to, place = member(kind, d)
            at = pl.ds(pl.multiple_of(place * size, size), size)
            out.append(remote(g, base + d, src.at[ks, at], dst.at[d - 1, ks], to))
        return out

    def first_copies(g):
        return split_copies(g, order(g)[2], 0, quarter, snd_a, rcv_a)

    def second_copies(g):
        return split_copies(g, order(g)[3], n_a, shard, snd_b, rcv_b)

    def beyond_copies(g):
        ks = pl.ds(*PARTS[g][:2])
        return [
            remote(g, n_a + n_b + d, rcv_c.at[beyond, ks], rcv_c.at[beyond, ks], copy_to(d))
            for d in range(1, copies)
        ]

    def gather_copies(g, kind, base, start, size):
        block = gat.at[core, pl.ds(*PARTS[g][:2]), pl.ds(start, size)]
        return [remote(g, base + d, block, block, member(kind, d)[0]) for d in range(1, count[kind])]

    def second_gather(g):
        return gather_copies(g, order(g)[3], n_a + n_b + n_c, second_at(g), shard)

    def first_gather(g):
        return gather_copies(g, order(g)[2], n_a + 2 * n_b + n_c, first_at(g), quarter)

    def core_gather(g):
        block = gat.at[core, pl.ds(*PARTS[g][:2])]
        return [remote(g, slots - 1, block, block, (lon, flip(lat, 1)))]

    def start(copies_of):
        for copy in copies_of:
            copy.start()

    def wait(copies_of):
        for copy in copies_of:
            copy.wait()

    def product(g):
        k0, kn = PARTS[g][:2]
        for k in range(k0, k0 + kn):
            part = nn_dot(inp_r[...], spread[:, k * chans : (k + 1) * chans])
            low, high = part[:, :LANES], part[:, LANES:]
            acc[k] = jnp.where(core == 0, low, high)
            snd0[k] = jnp.where(core == 0, high, low).astype(BF16)
        start(core_copies(g))

    def k_slice(g):
        return slice(PARTS[g][0], PARTS[g][0] + PARTS[g][1])

    def core_sum(g):
        wait(core_copies(g))
        ks = k_slice(g)
        snd_a[ks] = (acc[ks] + rcv0[ks].astype(F32)).astype(BF16)
        start(first_copies(g))
        at = pl.ds(first_at(g), quarter)
        acc_a[ks] = acc[ks, at] + rcv0[ks, at].astype(F32)

    def first_sum(g):
        wait(first_copies(g))
        ks = k_slice(g)
        total = acc_a[ks]
        for d in range(count[order(g)[2]] - 1):
            total += rcv_a[d, ks].astype(F32)
        snd_b[ks] = total.astype(BF16)
        start(second_copies(g))
        acc_b[ks] = total

    def second_sum(g):
        wait(second_copies(g))
        ks = k_slice(g)
        total = acc_b[ks, pl.ds(pl.multiple_of(mine[order(g)[3]] * shard, shard), shard)]
        for d in range(count[order(g)[3]] - 1):
            total += rcv_b[d, ks].astype(F32)
        if copies > 1:
            rcv_c[beyond, ks] = total.astype(BF16)
            start(beyond_copies(g))
            wait(beyond_copies(g))
            total = rcv_c[0, ks].astype(F32)
            for d in range(1, copies):
                total += rcv_c[d, ks].astype(F32)
        gat[core, ks, pl.ds(second_at(g), shard)] = total.astype(BF16)
        start(second_gather(g))

    def second_done(g):
        wait(second_gather(g))
        start(first_gather(g))

    def first_done(g):
        wait(first_gather(g))
        start(core_gather(g))

    def wg_store(g):
        ks = pl.ds(*PARTS[g][:2])
        return pltpu.make_async_copy(gat.at[:, ks], wg_hbm.at[:, ks], out_sem.at[g])

    def core_done(g):
        wait(core_gather(g))
        wg_store(g).start()

    def ig_part(r):
        at = slice(r * cols, (r + 1) * cols)
        part = nn_dot(spread[at, :], mix_v[...]).astype(BF16)
        ig_row[r] = nt_dot(eye, part).astype(BF16)

    def ig_final(b):
        part = jnp.concatenate([ig_row[r, b * group : (b + 1) * group, :] for r in range(rows)], axis=0)
        ig_v[b * chans : (b + 1) * chans, :] = nn_dot(scatter, part).astype(BF16)

    ig_store = pltpu.make_async_copy(ig_v, ig_hbm, out_sem.at[GROUPS])

    side_work = [functools.partial(ig_part, r) for r in range(rows)]
    side_work += [functools.partial(ig_final, b) for b in range(rows)] + [ig_store.start]

    steps = []
    for g in range(GROUPS):
        for s, step in enumerate((core_sum, first_sum, second_sum, second_done, first_done, core_done)):
            steps.append((PACE * s + g, s, functools.partial(step, g)))
    steps.sort(key=lambda item: item[:2])

    loads[3].wait()
    edge_blocks(0, kernels)
    for g in range(GROUPS):
        product(g)
        if g > 0 and steps[0][1] == 0:
            steps.pop(0)[2]()
    steps = [step for _, _, step in steps]
    for i, step in enumerate(steps):
        if side_work:
            side_work.pop(0)()
        step()
    for work in side_work:
        work()
    for g in range(GROUPS):
        wg_store(g).wait()
    ig_store.wait()


def finish(scale, gat_v, ig_v, wg_hbm, out_hbm, wg_v, wg_sem, ig_sem):
    _, kernels, chans, _ = gat_v.shape
    ig_out = pltpu.make_async_copy(ig_v, out_hbm, ig_sem)
    at0 = lax.broadcasted_iota(jnp.int32, (LANES, LANES), 0)
    at1 = lax.broadcasted_iota(jnp.int32, (LANES, LANES), 1)
    eye = (at0 == at1).astype(BF16)
    stores = []
    pieces = math.gcd(kernels, 3)
    per = kernels // pieces
    for g in range(pieces):
        for k in range(g * per, (g + 1) * per):
            for h in range(chans // LANES):
                start = k * chans + h * LANES
                wg_v[start : start + LANES, :] = nt_dot(eye, gat_v[h, k]) * scale
        rows = pl.ds(g * per * chans, per * chans)
        stores.append(pltpu.make_async_copy(wg_v.at[rows], wg_hbm.at[rows], wg_sem.at[g]))
        stores[-1].start()
        if g == 0:
            ig_out.start()
    for store in stores:
        store.wait()
    ig_out.wait()


def local(nlon, nlat, inputs, cotangent, mixing, filters, support):
    chans, rows, cols = inputs.shape
    kernels = filters.shape[0]
    plane, line, copies = layout(nlon, nlat)
    quarter, shard = chans // plane, chans // (plane * line)
    slots = GROUPS * (2 + 2 * (plane - 1) + 2 * (line - 1) + copies - 1)
    any_spec = pl.BlockSpec(memory_space=pl.ANY)
    vm = pltpu.VMEM
    flops = 2 * rows * cols * kernels * chans * chans * 3
    ig, wg = pl.pallas_call(
        functools.partial(kernel, nlon, nlat, kernels, chans, rows, cols),
        out_shape=(
            jax.ShapeDtypeStruct((chans * rows, cols), BF16),
            jax.ShapeDtypeStruct((2, kernels, chans, LANES), BF16),
        ),
        in_specs=[any_spec] * 5,
        out_specs=(any_spec, any_spec),
        scratch_shapes=[
            vm((chans * rows, cols), BF16),
            vm((chans * rows, cols), BF16),
            vm((kernels * chans, chans), BF16),
            vm((kernels * ROWS_A * rows, TAPS), BF16),
            pltpu.SMEM((rows,), jnp.int32),
            vm((rows + 2, TILE, DEPTH), BF16),
            vm((2, TILE, DEPTH), BF16),
            vm((rows, chans, cols), BF16),
            vm((chans, rows * cols), BF16),
            vm((rows + 2, cols + 2 * LON_REACH, chans), BF16),
            vm((rows, kernels * BLOCK, DEPTH), BF16),
            vm((rows * cols, kernels * chans), BF16),
            vm((kernels, chans, LANES), F32),
            vm((kernels, chans, LANES), BF16),
            vm((kernels, chans, LANES), BF16),
            vm((kernels, chans, LANES), BF16),
            vm((kernels, quarter, LANES), F32),
            vm((plane - 1, kernels, quarter, LANES), BF16),
            vm((kernels, quarter, LANES), BF16),
            vm((kernels, quarter, LANES), F32),
            vm((line - 1, kernels, shard, LANES), BF16),
            vm((copies, kernels, shard, LANES), BF16),
            vm((2, kernels, chans, LANES), BF16),
            vm((rows, chans, cols), BF16),
            vm((chans * rows, cols), BF16),
            pltpu.SemaphoreType.DMA((5,)),
            pltpu.SemaphoreType.DMA((GROUPS + 1,)),
            pltpu.SemaphoreType.DMA((10,)),
            pltpu.SemaphoreType.DMA((10,)),
            pltpu.SemaphoreType.DMA((slots,)),
            pltpu.SemaphoreType.DMA((slots,)),
        ],
        compiler_params=pltpu.CompilerParams(
            collective_id=0, has_side_effects=True, vmem_limit_bytes=32 * 2**20
        ),
        cost_estimate=pl.CostEstimate(flops=flops, bytes_accessed=7 * 2**20, transcendentals=0),
    )(
        pltpu.with_memory_space_constraint(cotangent.reshape(chans * rows, cols), pltpu.HBM),
        pltpu.with_memory_space_constraint(inputs.reshape(chans * rows, cols), pltpu.HBM),
        pltpu.with_memory_space_constraint(mixing.reshape(kernels * chans, chans), pltpu.HBM),
        pltpu.with_memory_space_constraint(jnp.transpose(filters, (0, 2, 1, 3)).reshape(kernels * ROWS_A * rows, TAPS), pltpu.HBM),
        pltpu.with_memory_space_constraint(support, pltpu.HBM),
    )
    scale = 1.0 / math.sqrt(rows * nlat * cols * nlon)
    weight_grad, input_grad = pl.pallas_call(
        functools.partial(finish, scale),
        out_shape=(
            jax.ShapeDtypeStruct((kernels * chans, chans), F32),
            jax.ShapeDtypeStruct((chans * rows, cols), BF16),
        ),
        in_specs=[pl.BlockSpec(memory_space=pltpu.VMEM)] * 2,
        out_specs=(any_spec, any_spec),
        scratch_shapes=[
            vm((kernels * chans, chans), F32),
            pltpu.SemaphoreType.DMA((kernels,)),
            pltpu.SemaphoreType.DMA,
        ],
        compiler_params=pltpu.CompilerParams(vmem_limit_bytes=16 * 2**20),
    )(wg, ig)
    return input_grad.reshape(chans, rows, cols), weight_grad.reshape(kernels, chans, chans)


def solution(mesh):
    return jax.shard_map(
        functools.partial(local, mesh.shape["lon"], mesh.shape["lat"]),
        mesh=mesh,
        in_specs=(
            P(None, "lat", "lon"),
            P(None, "lat", "lon"),
            P(),
            P(None, "lat", None, None),
            P("lat"),
        ),
        out_specs=(P(None, "lat", "lon"), P()),
        check_vma=False,
    )
```

```python
import functools
import math

import jax
import jax.numpy as jnp
from jax import lax
from jax.experimental import pallas as pl
from jax.experimental.pallas import tpu as pltpu
from jax.sharding import PartitionSpec as P

LAT_REACH = 1
LON_REACH = 16
TAPS = 2 * LON_REACH + 1
ROWS_A = 2 * LAT_REACH + 1
BLOCK = 48
WINDOW = BLOCK + 2 * LON_REACH
DEPTH = 256
TILE = 16
LANES = 128
QUARTER = 4
PARTS = ((0, 2, "plane"), (2, 4, "plane"), (6, 3, "line"))
GROUPS = len(PARTS)
PACE = 2

F32 = jnp.float32
BF16 = jnp.bfloat16
MESH = pl.DeviceIdType.MESH


def nt_dot(a, b):
    return lax.dot_general(a, b, (((1,), (1,)), ((), ())), preferred_element_type=F32)


def nn_dot(a, b):
    return lax.dot_general(a, b, (((1,), (0,)), ((), ())), preferred_element_type=F32)


def flip(index, step):
    return index + step - 2 * step * ((index // step) % 2)


def layout(nlon, nlat):
    copies = (nlon // (2 * QUARTER)) * (nlat // QUARTER)
    return QUARTER, QUARTER, copies


def kernel(
    nlon, nlat, kernels, chans, rows, cols,
    cot_hbm, inp_hbm, mix_hbm, filt_hbm, support_hbm, ig_v, gat,
    cot_v, inp_v, mix_v, filt_v, support, taps_v, taps_x, by_row, inp_m, inp_x, cot_t, toep, spread, spread_x,
    acc_m, acc, snd0, rcv0, snd_a, acc_a, rcv_a, snd_b, acc_b, rcv_b, rcv_c, ig_row,
    in_sem, halo_send, halo_recv, ar_send, ar_recv,
):
    lon, lat = lax.axis_index("lon"), lax.axis_index("lat")
    core = lat % 2
    plane, line, copies = layout(nlon, nlat)

    loads = [
        pltpu.make_async_copy(cot_hbm, cot_v, in_sem.at[0]),
        pltpu.make_async_copy(filt_hbm, filt_v, in_sem.at[1]),
        pltpu.make_async_copy(inp_hbm, inp_v, in_sem.at[2]),
        pltpu.make_async_copy(mix_hbm, mix_v, in_sem.at[3]),
        pltpu.make_async_copy(support_hbm, support, in_sem.at[4]),
    ]
    for load in loads:
        load.start()

    lon_down, lon_up = (lon + nlon - 1) % nlon, (lon + 1) % nlon
    has_above, has_below = lat > 0, lat < nlat - 1

    x, y = lon % 2, (lat // 2) % 2
    z = (lon // 2) % line
    beyond = (lon // (2 * line)) * (nlat // 4) + lat // 4

    def plane_to(d):
        return (flip(lon, 1) if d % 2 else lon), (flip(lat, 2) if d // 2 else lat)

    def line_to(d):
        return lon + 2 * ((z + d) % line - z), lat

    def copy_to(d):
        to = (beyond + d) % copies
        lon_to = (to // (nlat // 4)) * (2 * line) + lon % (2 * line)
        return lon_to, (to % (nlat // 4)) * 4 + lat % 4

    barrier = pltpu.get_barrier_semaphore()

    def greet(lon_to, lat_to):
        pl.semaphore_signal(
            barrier, inc=1, device_id={"lon": lon_to, "lat": lat_to}, device_id_type=MESH
        )

    partners = [plane_to(d) for d in range(1, plane)] + [line_to(d) for d in range(1, line)]
    partners += [copy_to(d) for d in range(1, copies)]

    greet(lon_down, lat)
    greet(lon_up, lat)

    @pl.when(has_above)
    def _():
        for lon_to in (lon_down, lon, lon_up):
            greet(lon_to, lat - 1)

    @pl.when(has_below)
    def _():
        for lon_to in (lon_down, lon, lon_up):
            greet(lon_to, lat + 1)

    for lon_to, lat_to in partners:
        greet(lon_to, lat_to)

    at0 = lax.broadcasted_iota(jnp.int32, (chans, chans), 0)
    at1 = lax.broadcasted_iota(jnp.int32, (chans, chans), 1)
    group = chans // rows
    eye = (at0 == at1).astype(BF16)
    gather = (at1 == (at0 % group) * rows + at0 // group).astype(BF16)
    scatter = (at0 == (at1 % group) * rows + at1 // group).astype(BF16)

    loads[1].wait()
    loads[4].wait()
    filt_rows = kernels * ROWS_A * rows
    lane = lax.broadcasted_iota(jnp.int32, (rows, TAPS), 1)
    sub = lax.broadcasted_iota(jnp.int32, (rows, TAPS), 0)
    reach = jnp.zeros((rows, TAPS), jnp.int32)
    for r in range(rows):
        reach = jnp.where(sub == r, support[r], reach)
    keep = (jnp.abs(lane - LON_REACH) <= reach).astype(F32)
    coefs = filt_v[...].astype(F32).reshape(kernels * ROWS_A, rows, TAPS) * keep[None]
    coefs = coefs.reshape(filt_rows, TAPS).astype(BF16)
    out_rows = (rows + 2) * TILE
    pick0 = lax.broadcasted_iota(jnp.int32, (out_rows, filt_rows), 0)
    pick1 = lax.broadcasted_iota(jnp.int32, (out_rows, filt_rows), 1)
    tap = lax.broadcasted_iota(jnp.int32, (TAPS, DEPTH), 0)
    spot = lax.broadcasted_iota(jnp.int32, (TAPS, DEPTH), 1)
    placed = jnp.zeros((out_rows, DEPTH), F32)
    for a in range(ROWS_A):
        row = pick0 // TILE - a
        k = pick0 % TILE
        pick = (pick1 == k * (ROWS_A * rows) + a * rows + row) & (row >= 0) & (row < rows) & (k < kernels)
        chosen = nn_dot(pick.astype(BF16), coefs).astype(BF16)
        placed += nn_dot(chosen, (spot == a * WINDOW + TAPS - 1 - tap).astype(BF16))
    taps_v[...] = placed.astype(BF16).reshape(rows + 2, TILE, DEPTH)

    @pl.when(jnp.logical_not(has_above))
    def _():
        cot_t[0] = jnp.zeros_like(cot_t[0])
        taps_x[0] = jnp.zeros_like(taps_x[0])

    @pl.when(jnp.logical_not(has_below))
    def _():
        cot_t[rows + 1] = jnp.zeros_like(cot_t[rows + 1])
        taps_x[1] = jnp.zeros_like(taps_x[1])

    loads[0].wait()
    for b in range(rows):
        part = nn_dot(gather, cot_v[b * chans : (b + 1) * chans, :]).astype(BF16)
        for r in range(rows):
            by_row[r, b * group : (b + 1) * group, :] = part[r * group : (r + 1) * group]
    for r in range(rows):
        cot_t[r + 1, LON_REACH : LON_REACH + cols, :] = nt_dot(eye, by_row[r]).astype(BF16)

    def widen(r, more=None):
        base = taps_v[r + 1].astype(F32)
        if more is not None:
            base += taps_x[more].astype(F32)
        for k in range(kernels):
            flat = jnp.broadcast_to(base[k : k + 1], (BLOCK, DEPTH))
            toep[r, k * BLOCK : (k + 1) * BLOCK, :] = pltpu.roll(
                flat, 0, 1, stride=1, stride_axis=0
            ).astype(BF16)

    reach_out = LON_REACH
    strips = [(0, 0, reach_out), (cols - BLOCK, BLOCK - reach_out, reach_out)]
    both = 2 * reach_out
    strip_rows = spread_x.shape[0] - 2 * cols
    middle = rows - 2
    for r in range(middle):
        for at in (r * cols, (r + 1) * cols - reach_out):
            spread[at : at + reach_out, :] = jnp.zeros((reach_out, kernels * chans), BF16)
    spare = strip_rows - middle * both
    if spare:
        spread_x[2 * cols + middle * both :, :] = jnp.zeros((spare, kernels * chans), BF16)

    loads[2].wait()
    for b in range(rows):
        part = nn_dot(gather, inp_v[b * chans : (b + 1) * chans, :]).astype(BF16)
        own_rows = slice(b * group, (b + 1) * group)
        for r in range(rows):
            piece = part[r * group : (r + 1) * group]
            if 0 < r < rows - 1:
                inp_m[own_rows, (r - 1) * cols : r * cols] = piece
            else:
                at = 0 if r == 0 else cols
                inp_x[own_rows, at : at + cols] = piece
    strip0 = lax.broadcasted_iota(jnp.int32, (cols, strip_rows), 0)
    strip1 = lax.broadcasted_iota(jnp.int32, (cols, strip_rows), 1)
    chosen = jnp.zeros((chans, strip_rows), F32)
    for r in range(middle):
        lead = (strip0 < reach_out) & (strip1 == strip0 + r * both)
        trail = (strip0 >= cols - reach_out) & (strip1 == strip0 + (r * both + both - cols))
        chosen += nn_dot(inp_m[:, r * cols : (r + 1) * cols], (lead | trail).astype(BF16))
    inp_x[:, 2 * cols :] = chosen.astype(BF16)

    pad = jnp.zeros((DEPTH - ROWS_A * WINDOW, chans), BF16)

    def spread_block(r, start, low, size):
        source = jnp.concatenate(
            [cot_t[r + 2 - a, start : start + WINDOW, :] for a in range(ROWS_A)] + [pad], axis=0
        )
        if size == BLOCK:
            bands = toep[r]
        else:
            bands = jnp.concatenate(
                [toep[r, k * BLOCK + low : k * BLOCK + low + size, :] for k in range(kernels)], axis=0
            )
        return nn_dot(bands, source).astype(BF16)

    def put(ref, at, out, size):
        for k in range(kernels):
            ref[pl.ds(at, size), k * chans : (k + 1) * chans] = out[k * size : (k + 1) * size]

    def cover(first, last):
        out = [(at, 0, BLOCK) for at in range(first, last - BLOCK + 1, BLOCK)]
        rest = (last - first) % BLOCK
        if rest:
            out.append((last - BLOCK, BLOCK - rest, rest))
        return out

    edges = has_above.astype(jnp.int32) + has_below.astype(jnp.int32)
    pl.semaphore_wait(barrier, 2 + len(partners) + 3 * edges)

    own = pl.ds(LON_REACH, cols)
    head, tail = pl.ds(LON_REACH, LON_REACH), pl.ds(cols, LON_REACH)
    left, right = pl.ds(0, LON_REACH), pl.ds(LON_REACH + cols, LON_REACH)
    every = pl.ds(1, rows)

    def halo(i, src, dst, lon_to, lat_to):
        return pltpu.make_async_remote_copy(
            src_ref=src, dst_ref=dst, send_sem=halo_send.at[i], recv_sem=halo_recv.at[i],
            device_id={"lon": lon_to, "lat": lat_to}, device_id_type=MESH,
        )

    sides = [
        halo(0, cot_t.at[every, head], cot_t.at[every, right], lon_down, lat),
        halo(1, cot_t.at[every, tail], cot_t.at[every, left], lon_up, lat),
    ]
    above, below = lat - 1, lat + 1
    upward = [
        halo(2, cot_t.at[1, own], cot_t.at[rows + 1, own], lon, above),
        halo(3, cot_t.at[1, head], cot_t.at[rows + 1, right], lon_down, above),
        halo(4, cot_t.at[1, tail], cot_t.at[rows + 1, left], lon_up, above),
        halo(5, taps_v.at[0], taps_x.at[1], lon, above),
    ]
    downward = [
        halo(6, cot_t.at[rows, own], cot_t.at[0, own], lon, below),
        halo(7, cot_t.at[rows, head], cot_t.at[0, right], lon_down, below),
        halo(8, cot_t.at[rows, tail], cot_t.at[0, left], lon_up, below),
        halo(9, taps_v.at[rows + 1], taps_x.at[0], lon, below),
    ]

    for copy in sides:
        copy.start()

    @pl.when(has_above)
    def _():
        for copy in upward:
            copy.start()

    @pl.when(has_below)
    def _():
        for copy in downward:
            copy.start()

    def inner_row(r, carry):
        widen(r)
        base = pl.multiple_of((r - 1) * cols, cols)
        for start, low, size in cover(reach_out, cols - reach_out):
            put(spread, base + start + low, spread_block(r, start, low, size), size)
        return carry

    lax.fori_loop(1, rows - 1, inner_row, 0)

    for k in range(kernels):
        acc_m[k] = nn_dot(inp_m[...], spread[:, k * chans : (k + 1) * chans])

    for copy in sides:
        copy.wait()

    def side_row(r, carry):
        base = pl.multiple_of((r - 1) * cols, cols)
        base_x = pl.multiple_of(2 * cols + (r - 1) * both, both)
        for i, (start, low, size) in enumerate(strips):
            out = spread_block(r, start, low, size)
            put(spread, base + start + low, out, size)
            put(spread_x, base_x + i * size, out, size)
        return carry

    lax.fori_loop(1, rows - 1, side_row, 0)

    @pl.when(has_above)
    def _():
        for copy in upward:
            copy.wait_send()
        for copy in downward:
            copy.wait_recv()

    @pl.when(has_below)
    def _():
        for copy in downward:
            copy.wait_send()
        for copy in upward:
            copy.wait_recv()

    widen(0, 0)
    widen(rows - 1, 1)

    def end_row(i, carry):
        base = pl.multiple_of(i * cols, cols)
        for start, low, size in cover(0, cols):
            put(spread_x, base + start + low, spread_block(i * (rows - 1), start, low, size), size)
        return carry

    lax.fori_loop(0, 2, end_row, 0)

    quarter, shard = chans // plane, chans // (plane * line)
    count = {"plane": plane, "line": line}
    turn = {"plane": (3, 1, 2), "line": (2, 1, 3)}
    mine = {"plane": x * 2 + y, "line": z}
    n_a, n_b, n_c = plane - 1, line - 1, copies - 1
    slots = 2 + 2 * n_a + 2 * n_b + n_c

    def member(kind, d):
        if kind == "line":
            return line_to(d), (z + d) % line
        x_to = flip(x, 1) if d % 2 else x
        y_to = flip(y, 1) if d // 2 else y
        return plane_to(d), x_to * 2 + y_to

    def order(g):
        k0, kn, one = PARTS[g]
        return k0, kn, one, ("line" if one == "plane" else "plane")

    def first_at(g):
        return pl.multiple_of(mine[order(g)[2]] * quarter, quarter)

    def second_at(g):
        return pl.multiple_of(mine[order(g)[2]] * quarter + mine[order(g)[3]] * shard, shard)

    def remote(g, slot, src, dst, to):
        at = g * slots + slot
        return pltpu.make_async_remote_copy(
            src_ref=src, dst_ref=dst, send_sem=ar_send.at[at], recv_sem=ar_recv.at[at],
            device_id={"lon": to[0], "lat": to[1]}, device_id_type=MESH,
        )

    def core_copies(g):
        ks = pl.ds(*PARTS[g][:2])
        return [remote(g, 0, snd0.at[ks], rcv0.at[ks], (lon, flip(lat, 1)))]

    def split_copies(g, kind, base, size, src, dst):
        ks, out = pl.ds(*PARTS[g][:2]), []
        for d in turn[kind]:
            to, place = member(kind, d)
            at = pl.ds(pl.multiple_of(place * size, size), size)
            out.append(remote(g, base + d, src.at[ks, at], dst.at[d - 1, ks], to))
        return out

    def first_copies(g):
        return split_copies(g, order(g)[2], 0, quarter, snd_a, rcv_a)

    def second_copies(g):
        return split_copies(g, order(g)[3], n_a, shard, snd_b, rcv_b)

    def beyond_copies(g):
        ks = pl.ds(*PARTS[g][:2])
        return [
            remote(g, n_a + n_b + d, rcv_c.at[beyond, ks], rcv_c.at[beyond, ks], copy_to(d))
            for d in range(1, copies)
        ]

    def gather_copies(g, kind, base, start, size):
        block = gat.at[core, pl.ds(*PARTS[g][:2]), pl.ds(start, size)]
        return [remote(g, base + d, block, block, member(kind, d)[0]) for d in turn[kind]]

    def second_gather(g):
        return gather_copies(g, order(g)[3], n_a + n_b + n_c, second_at(g), shard)

    def first_gather(g):
        return gather_copies(g, order(g)[2], n_a + 2 * n_b + n_c, first_at(g), quarter)

    def core_gather(g):
        block = gat.at[core, pl.ds(*PARTS[g][:2])]
        return [remote(g, slots - 1, block, block, (lon, flip(lat, 1)))]

    def start(copies_of):
        for copy in copies_of:
            copy.start()

    def wait(copies_of):
        for copy in copies_of:
            copy.wait()

    def product(g):
        k0, kn = PARTS[g][:2]
        for k in range(k0, k0 + kn):
            part = acc_m[k] + nn_dot(inp_x[...], spread_x[:, k * chans : (k + 1) * chans])
            low, high = part[:, :LANES], part[:, LANES:]
            acc[k] = jnp.where(core == 0, low, high)
            snd0[k] = jnp.where(core == 0, high, low).astype(BF16)
        start(core_copies(g))

    def k_slice(g):
        return slice(PARTS[g][0], PARTS[g][0] + PARTS[g][1])

    def core_sum(g):
        wait(core_copies(g))
        ks = k_slice(g)
        snd_a[ks] = (acc[ks] + rcv0[ks].astype(F32)).astype(BF16)
        start(first_copies(g))
        at = pl.ds(first_at(g), quarter)
        acc_a[ks] = acc[ks, at] + rcv0[ks, at].astype(F32)

    def first_sum(g):
        wait(first_copies(g))
        ks = k_slice(g)
        total = acc_a[ks]
        for d in range(count[order(g)[2]] - 1):
            total += rcv_a[d, ks].astype(F32)
        snd_b[ks] = total.astype(BF16)
        start(second_copies(g))
        acc_b[ks] = total

    def second_sum(g):
        wait(second_copies(g))
        ks = k_slice(g)
        total = acc_b[ks, pl.ds(pl.multiple_of(mine[order(g)[3]] * shard, shard), shard)]
        for d in range(count[order(g)[3]] - 1):
            total += rcv_b[d, ks].astype(F32)
        if copies > 1:
            rcv_c[beyond, ks] = total.astype(BF16)
            start(beyond_copies(g))
            wait(beyond_copies(g))
            total = rcv_c[0, ks].astype(F32)
            for d in range(1, copies):
                total += rcv_c[d, ks].astype(F32)
        gat[core, ks, pl.ds(second_at(g), shard)] = total.astype(BF16)
        start(second_gather(g))

    def second_done(g):
        wait(second_gather(g))
        start(first_gather(g))

    def first_done(g):
        wait(first_gather(g))
        start(core_gather(g))

    def core_done(g):
        wait(core_gather(g))

    def ig_part(r):
        if 0 < r < rows - 1:
            source = spread[(r - 1) * cols : r * cols, :]
        else:
            at = 0 if r == 0 else cols
            source = spread_x[at : at + cols, :]
        part = nn_dot(source, mix_v[...]).astype(BF16)
        ig_row[r] = nt_dot(eye, part).astype(BF16)

    def ig_final(b):
        part = jnp.concatenate([ig_row[r, b * group : (b + 1) * group, :] for r in range(rows)], axis=0)
        ig_v[b * chans : (b + 1) * chans, :] = nn_dot(scatter, part).astype(BF16)

    side_work = [functools.partial(ig_part, r) for r in range(rows)]
    side_work += [functools.partial(ig_final, b) for b in range(rows)]

    steps = []
    for g in range(GROUPS):
        for s, step in enumerate((core_sum, first_sum, second_sum, second_done, first_done, core_done)):
            steps.append((PACE * s + g, s, functools.partial(step, g)))
    steps.sort(key=lambda item: item[:2])

    loads[3].wait()
    for g in range(GROUPS):
        product(g)
        if g > 0 and steps[0][1] == 0:
            steps.pop(0)[2]()
    steps = [step for _, _, step in steps]
    for i, step in enumerate(steps):
        if side_work:
            side_work.pop(0)()
        step()
    for work in side_work:
        work()


def finish(scale, gat_v, ig_v, wg_hbm, out_hbm, wg_v, wg_sem, ig_sem):
    _, kernels, chans, _ = gat_v.shape
    ig_out = pltpu.make_async_copy(ig_v, out_hbm, ig_sem)
    at0 = lax.broadcasted_iota(jnp.int32, (LANES, LANES), 0)
    at1 = lax.broadcasted_iota(jnp.int32, (LANES, LANES), 1)
    eye = (at0 == at1).astype(BF16)
    ig_out.start()
    stores = []
    pieces = math.gcd(kernels, 3)
    per = kernels // pieces
    for g in range(pieces):
        for k in range(g * per, (g + 1) * per):
            for h in range(chans // LANES):
                start = k * chans + h * LANES
                wg_v[start : start + LANES, :] = nt_dot(eye, gat_v[h, k]) * scale
        rows = pl.ds(g * per * chans, per * chans)
        stores.append(pltpu.make_async_copy(wg_v.at[rows], wg_hbm.at[rows], wg_sem.at[g]))
        stores[-1].start()
    for store in stores:
        store.wait()
    ig_out.wait()


def local(nlon, nlat, inputs, cotangent, mixing, filters, support):
    chans, rows, cols = inputs.shape
    kernels = filters.shape[0]
    plane, line, copies = layout(nlon, nlat)
    quarter, shard = chans // plane, chans // (plane * line)
    slots = GROUPS * (2 + 2 * (plane - 1) + 2 * (line - 1) + copies - 1)
    strip_rows = -(-(rows - 2) * 2 * LON_REACH // DEPTH) * DEPTH
    any_spec = pl.BlockSpec(memory_space=pl.ANY)
    vm = pltpu.VMEM
    flops = 2 * rows * cols * kernels * chans * chans * 3
    ig, wg = pl.pallas_call(
        functools.partial(kernel, nlon, nlat, kernels, chans, rows, cols),
        out_shape=(
            jax.ShapeDtypeStruct((chans * rows, cols), BF16),
            jax.ShapeDtypeStruct((2, kernels, chans, LANES), BF16),
        ),
        in_specs=[any_spec] * 5,
        out_specs=[pl.BlockSpec(memory_space=pltpu.VMEM)] * 2,
        scratch_shapes=[
            vm((chans * rows, cols), BF16),
            vm((chans * rows, cols), BF16),
            vm((kernels * chans, chans), BF16),
            vm((kernels * ROWS_A * rows, TAPS), BF16),
            pltpu.SMEM((rows,), jnp.int32),
            vm((rows + 2, TILE, DEPTH), BF16),
            vm((2, TILE, DEPTH), BF16),
            vm((rows, chans, cols), BF16),
            vm((chans, (rows - 2) * cols), BF16),
            vm((chans, 2 * cols + strip_rows), BF16),
            vm((rows + 2, cols + 2 * LON_REACH, chans), BF16),
            vm((rows, kernels * BLOCK, DEPTH), BF16),
            vm(((rows - 2) * cols, kernels * chans), BF16),
            vm((2 * cols + strip_rows, kernels * chans), BF16),
            vm((kernels, chans, chans), F32),
            vm((kernels, chans, LANES), F32),
            vm((kernels, chans, LANES), BF16),
            vm((kernels, chans, LANES), BF16),
            vm((kernels, chans, LANES), BF16),
            vm((kernels, quarter, LANES), F32),
            vm((plane - 1, kernels, quarter, LANES), BF16),
            vm((kernels, quarter, LANES), BF16),
            vm((kernels, quarter, LANES), F32),
            vm((line - 1, kernels, shard, LANES), BF16),
            vm((copies, kernels, shard, LANES), BF16),
            vm((rows, chans, cols), BF16),
            pltpu.SemaphoreType.DMA((5,)),
            pltpu.SemaphoreType.DMA((10,)),
            pltpu.SemaphoreType.DMA((10,)),
            pltpu.SemaphoreType.DMA((slots,)),
            pltpu.SemaphoreType.DMA((slots,)),
        ],
        compiler_params=pltpu.CompilerParams(
            collective_id=0, has_side_effects=True, vmem_limit_bytes=40 * 2**20
        ),
        cost_estimate=pl.CostEstimate(flops=flops, bytes_accessed=7 * 2**20, transcendentals=0),
    )(
        pltpu.with_memory_space_constraint(cotangent.reshape(chans * rows, cols), pltpu.HBM),
        pltpu.with_memory_space_constraint(inputs.reshape(chans * rows, cols), pltpu.HBM),
        pltpu.with_memory_space_constraint(mixing.reshape(kernels * chans, chans), pltpu.HBM),
        pltpu.with_memory_space_constraint(jnp.transpose(filters, (0, 2, 1, 3)).reshape(kernels * ROWS_A * rows, TAPS), pltpu.HBM),
        pltpu.with_memory_space_constraint(support, pltpu.HBM),
    )
    scale = 1.0 / math.sqrt(rows * nlat * cols * nlon)
    weight_grad, input_grad = pl.pallas_call(
        functools.partial(finish, scale),
        out_shape=(
            jax.ShapeDtypeStruct((kernels * chans, chans), F32),
            jax.ShapeDtypeStruct((chans * rows, cols), BF16),
        ),
        in_specs=[pl.BlockSpec(memory_space=pltpu.VMEM)] * 2,
        out_specs=(any_spec, any_spec),
        scratch_shapes=[
            vm((kernels * chans, chans), F32),
            pltpu.SemaphoreType.DMA((kernels,)),
            pltpu.SemaphoreType.DMA,
        ],
        compiler_params=pltpu.CompilerParams(vmem_limit_bytes=16 * 2**20),
    )(wg, ig)
    return input_grad.reshape(chans, rows, cols), weight_grad.reshape(kernels, chans, chans)


def solution(mesh):
    return jax.shard_map(
        functools.partial(local, mesh.shape["lon"], mesh.shape["lat"]),
        mesh=mesh,
        in_specs=(
            P(None, "lat", "lon"),
            P(None, "lat", "lon"),
            P(),
            P(None, "lat", None, None),
            P("lat"),
        ),
        out_specs=(P(None, "lat", "lon"), P()),
        check_vma=False,
    )
```

```python
import functools
import math

import jax
import jax.numpy as jnp
from jax import lax
from jax.experimental import pallas as pl
from jax.experimental.pallas import tpu as pltpu
from jax.sharding import PartitionSpec as P

LAT_REACH = 1
LON_REACH = 16
TAPS = 2 * LON_REACH + 1
ROWS_A = 2 * LAT_REACH + 1
BLOCK = 48
WINDOW = BLOCK + 2 * LON_REACH
DEPTH = 256
TILE = 16
LANES = 128
QUARTER = 4
PARTS = ((0, 2, "plane"), (2, 4, "plane"), (6, 3, "line"))
GROUPS = len(PARTS)
PACE = 2

F32 = jnp.float32
BF16 = jnp.bfloat16
MESH = pl.DeviceIdType.MESH


def nt_dot(a, b):
    return lax.dot_general(a, b, (((1,), (1,)), ((), ())), preferred_element_type=F32)


def nn_dot(a, b):
    return lax.dot_general(a, b, (((1,), (0,)), ((), ())), preferred_element_type=F32)


def flip(index, step):
    return index + step - 2 * step * ((index // step) % 2)


def layout(nlon, nlat):
    copies = (nlon // (2 * QUARTER)) * (nlat // QUARTER)
    return QUARTER, QUARTER, copies


def kernel(
    nlon, nlat, kernels, chans, rows, cols,
    cot_hbm, inp_hbm, mix_hbm, filt_hbm, support_hbm, ig_v, gat,
    cot_v, inp_v, mix_v, filt_v, support, taps_v, taps_x, by_row, inp_m, inp_x, cot_t, toep, spread, spread_x,
    acc_m, acc, snd0, rcv0, snd_a, acc_a, rcv_a, snd_b, acc_b, rcv_b, rcv_c, ig_row,
    in_sem, halo_send, halo_recv, ar_send, ar_recv,
):
    lon, lat = lax.axis_index("lon"), lax.axis_index("lat")
    core = lat % 2
    plane, line, copies = layout(nlon, nlat)

    loads = [
        pltpu.make_async_copy(cot_hbm, cot_v, in_sem.at[0]),
        pltpu.make_async_copy(filt_hbm, filt_v, in_sem.at[1]),
        pltpu.make_async_copy(inp_hbm, inp_v, in_sem.at[2]),
        pltpu.make_async_copy(mix_hbm, mix_v, in_sem.at[3]),
        pltpu.make_async_copy(support_hbm, support, in_sem.at[4]),
    ]
    for load in loads:
        load.start()

    lon_down, lon_up = (lon + nlon - 1) % nlon, (lon + 1) % nlon
    has_above, has_below = lat > 0, lat < nlat - 1

    x, y = lon % 2, (lat // 2) % 2
    z = (lon // 2) % line
    beyond = (lon // (2 * line)) * (nlat // 4) + lat // 4

    def plane_to(d):
        return (flip(lon, 1) if d % 2 else lon), (flip(lat, 2) if d // 2 else lat)

    def line_to(d):
        return lon + 2 * ((z + d) % line - z), lat

    def copy_to(d):
        to = (beyond + d) % copies
        lon_to = (to // (nlat // 4)) * (2 * line) + lon % (2 * line)
        return lon_to, (to % (nlat // 4)) * 4 + lat % 4

    barrier = pltpu.get_barrier_semaphore()

    def greet(lon_to, lat_to):
        pl.semaphore_signal(
            barrier, inc=1, device_id={"lon": lon_to, "lat": lat_to}, device_id_type=MESH
        )

    partners = [plane_to(d) for d in range(1, plane)] + [line_to(d) for d in range(1, line)]
    partners += [copy_to(d) for d in range(1, copies)]

    greet(lon_down, lat)
    greet(lon_up, lat)

    @pl.when(has_above)
    def _():
        for lon_to in (lon_down, lon, lon_up):
            greet(lon_to, lat - 1)

    @pl.when(has_below)
    def _():
        for lon_to in (lon_down, lon, lon_up):
            greet(lon_to, lat + 1)

    for lon_to, lat_to in partners:
        greet(lon_to, lat_to)

    at0 = lax.broadcasted_iota(jnp.int32, (chans, chans), 0)
    at1 = lax.broadcasted_iota(jnp.int32, (chans, chans), 1)
    group = chans // rows
    eye = (at0 == at1).astype(BF16)
    gather = (at1 == (at0 % group) * rows + at0 // group).astype(BF16)
    scatter = (at0 == (at1 % group) * rows + at1 // group).astype(BF16)

    loads[1].wait()
    loads[4].wait()
    filt_rows = kernels * ROWS_A * rows
    lane = lax.broadcasted_iota(jnp.int32, (rows, TAPS), 1)
    sub = lax.broadcasted_iota(jnp.int32, (rows, TAPS), 0)
    reach = jnp.zeros((rows, TAPS), jnp.int32)
    for r in range(rows):
        reach = jnp.where(sub == r, support[r], reach)
    keep = (jnp.abs(lane - LON_REACH) <= reach).astype(F32)
    coefs = filt_v[...].astype(F32).reshape(kernels * ROWS_A, rows, TAPS) * keep[None]
    coefs = coefs.reshape(filt_rows, TAPS).astype(BF16)
    out_rows = (rows + 2) * TILE
    pick0 = lax.broadcasted_iota(jnp.int32, (out_rows, filt_rows), 0)
    pick1 = lax.broadcasted_iota(jnp.int32, (out_rows, filt_rows), 1)
    tap = lax.broadcasted_iota(jnp.int32, (TAPS, DEPTH), 0)
    spot = lax.broadcasted_iota(jnp.int32, (TAPS, DEPTH), 1)
    placed = jnp.zeros((out_rows, DEPTH), F32)
    for a in range(ROWS_A):
        row = pick0 // TILE - a
        k = pick0 % TILE
        pick = (pick1 == k * (ROWS_A * rows) + a * rows + row) & (row >= 0) & (row < rows) & (k < kernels)
        chosen = nn_dot(pick.astype(BF16), coefs).astype(BF16)
        placed += nn_dot(chosen, (spot == a * WINDOW + TAPS - 1 - tap).astype(BF16))
    taps_v[...] = placed.astype(BF16).reshape(rows + 2, TILE, DEPTH)

    @pl.when(jnp.logical_not(has_above))
    def _():
        cot_t[0] = jnp.zeros_like(cot_t[0])
        taps_x[0] = jnp.zeros_like(taps_x[0])

    @pl.when(jnp.logical_not(has_below))
    def _():
        cot_t[rows + 1] = jnp.zeros_like(cot_t[rows + 1])
        taps_x[1] = jnp.zeros_like(taps_x[1])

    loads[0].wait()
    for b in range(rows):
        part = nn_dot(gather, cot_v[b * chans : (b + 1) * chans, :]).astype(BF16)
        for r in range(rows):
            by_row[r, b * group : (b + 1) * group, :] = part[r * group : (r + 1) * group]
    for r in range(rows):
        cot_t[r + 1, LON_REACH : LON_REACH + cols, :] = nt_dot(eye, by_row[r]).astype(BF16)

    def widen(r, more=None):
        base = taps_v[r + 1].astype(F32)
        if more is not None:
            base += taps_x[more].astype(F32)
        for k in range(kernels):
            flat = jnp.broadcast_to(base[k : k + 1], (BLOCK, DEPTH))
            toep[r, k * BLOCK : (k + 1) * BLOCK, :] = pltpu.roll(
                flat, 0, 1, stride=1, stride_axis=0
            ).astype(BF16)

    reach_out = LON_REACH
    strips = [(0, 0, reach_out), (cols - BLOCK, BLOCK - reach_out, reach_out)]
    both = 2 * reach_out
    strip_rows = spread_x.shape[0] - 2 * cols
    middle = rows - 2
    for r in range(middle):
        for at in (r * cols, (r + 1) * cols - reach_out):
            spread[at : at + reach_out, :] = jnp.zeros((reach_out, kernels * chans), BF16)
    spare = strip_rows - middle * both
    if spare:
        spread_x[2 * cols + middle * both :, :] = jnp.zeros((spare, kernels * chans), BF16)

    loads[2].wait()
    for b in range(rows):
        part = nn_dot(gather, inp_v[b * chans : (b + 1) * chans, :]).astype(BF16)
        own_rows = slice(b * group, (b + 1) * group)
        for r in range(rows):
            piece = part[r * group : (r + 1) * group]
            if 0 < r < rows - 1:
                inp_m[own_rows, (r - 1) * cols : r * cols] = piece
            else:
                at = 0 if r == 0 else cols
                inp_x[own_rows, at : at + cols] = piece
    strip0 = lax.broadcasted_iota(jnp.int32, (cols, strip_rows), 0)
    strip1 = lax.broadcasted_iota(jnp.int32, (cols, strip_rows), 1)
    chosen = jnp.zeros((chans, strip_rows), F32)
    for r in range(middle):
        lead = (strip0 < reach_out) & (strip1 == strip0 + r * both)
        trail = (strip0 >= cols - reach_out) & (strip1 == strip0 + (r * both + both - cols))
        chosen += nn_dot(inp_m[:, r * cols : (r + 1) * cols], (lead | trail).astype(BF16))
    inp_x[:, 2 * cols :] = chosen.astype(BF16)

    pad = jnp.zeros((DEPTH - ROWS_A * WINDOW, chans), BF16)

    def spread_block(r, start, low, size):
        source = jnp.concatenate(
            [cot_t[r + 2 - a, start : start + WINDOW, :] for a in range(ROWS_A)] + [pad], axis=0
        )
        if size == BLOCK:
            bands = toep[r]
        else:
            bands = jnp.concatenate(
                [toep[r, k * BLOCK + low : k * BLOCK + low + size, :] for k in range(kernels)], axis=0
            )
        return nn_dot(bands, source).astype(BF16)

    def put(ref, at, out, size):
        for k in range(kernels):
            ref[pl.ds(at, size), k * chans : (k + 1) * chans] = out[k * size : (k + 1) * size]

    def cover(first, last):
        out = [(at, 0, BLOCK) for at in range(first, last - BLOCK + 1, BLOCK)]
        rest = (last - first) % BLOCK
        if rest:
            out.append((last - BLOCK, BLOCK - rest, rest))
        return out

    edges = has_above.astype(jnp.int32) + has_below.astype(jnp.int32)
    pl.semaphore_wait(barrier, 2 + len(partners) + 3 * edges)

    own = pl.ds(LON_REACH, cols)
    head, tail = pl.ds(LON_REACH, LON_REACH), pl.ds(cols, LON_REACH)
    left, right = pl.ds(0, LON_REACH), pl.ds(LON_REACH + cols, LON_REACH)
    every = pl.ds(1, rows)

    def halo(i, src, dst, lon_to, lat_to):
        return pltpu.make_async_remote_copy(
            src_ref=src, dst_ref=dst, send_sem=halo_send.at[i], recv_sem=halo_recv.at[i],
            device_id={"lon": lon_to, "lat": lat_to}, device_id_type=MESH,
        )

    sides = [
        halo(0, cot_t.at[every, head], cot_t.at[every, right], lon_down, lat),
        halo(1, cot_t.at[every, tail], cot_t.at[every, left], lon_up, lat),
    ]
    above, below = lat - 1, lat + 1
    upward = [
        halo(2, cot_t.at[1, own], cot_t.at[rows + 1, own], lon, above),
        halo(3, cot_t.at[1, head], cot_t.at[rows + 1, right], lon_down, above),
        halo(4, cot_t.at[1, tail], cot_t.at[rows + 1, left], lon_up, above),
        halo(5, taps_v.at[0], taps_x.at[1], lon, above),
    ]
    downward = [
        halo(6, cot_t.at[rows, own], cot_t.at[0, own], lon, below),
        halo(7, cot_t.at[rows, head], cot_t.at[0, right], lon_down, below),
        halo(8, cot_t.at[rows, tail], cot_t.at[0, left], lon_up, below),
        halo(9, taps_v.at[rows + 1], taps_x.at[0], lon, below),
    ]

    for copy in sides:
        copy.start()

    @pl.when(has_above)
    def _():
        for copy in upward:
            copy.start()

    @pl.when(has_below)
    def _():
        for copy in downward:
            copy.start()

    def inner_row(r, carry):
        widen(r)
        base = pl.multiple_of((r - 1) * cols, cols)
        for start, low, size in cover(reach_out, cols - reach_out):
            put(spread, base + start + low, spread_block(r, start, low, size), size)
        return carry

    lax.fori_loop(1, rows - 1, inner_row, 0)

    for k in range(kernels):
        acc_m[k] = nn_dot(inp_m[...], spread[:, k * chans : (k + 1) * chans])

    for copy in sides:
        copy.wait()

    def side_row(r, carry):
        base = pl.multiple_of((r - 1) * cols, cols)
        base_x = pl.multiple_of(2 * cols + (r - 1) * both, both)
        for i, (start, low, size) in enumerate(strips):
            out = spread_block(r, start, low, size)
            put(spread, base + start + low, out, size)
            put(spread_x, base_x + i * size, out, size)
        return carry

    lax.fori_loop(1, rows - 1, side_row, 0)

    @pl.when(has_above)
    def _():
        for copy in upward:
            copy.wait_send()
        for copy in downward:
            copy.wait_recv()

    @pl.when(has_below)
    def _():
        for copy in downward:
            copy.wait_send()
        for copy in upward:
            copy.wait_recv()

    widen(0, 0)
    widen(rows - 1, 1)

    def end_row(i, carry):
        base = pl.multiple_of(i * cols, cols)
        for start, low, size in cover(0, cols):
            put(spread_x, base + start + low, spread_block(i * (rows - 1), start, low, size), size)
        return carry

    lax.fori_loop(0, 2, end_row, 0)

    quarter, shard = chans // plane, chans // (plane * line)
    count = {"plane": plane, "line": line}
    turn = {"plane": (3, 1, 2), "line": (2, 1, 3)}
    mine = {"plane": x * 2 + y, "line": z}
    n_a, n_b, n_c = plane - 1, line - 1, copies - 1
    slots = 1 + plane + 2 * n_a + 2 * n_b + n_c

    def member(kind, d):
        if kind == "line":
            return line_to(d), (z + d) % line
        x_to = flip(x, 1) if d % 2 else x
        y_to = flip(y, 1) if d // 2 else y
        return plane_to(d), x_to * 2 + y_to

    def order(g):
        k0, kn, one = PARTS[g]
        return k0, kn, one, ("line" if one == "plane" else "plane")

    def first_at(g):
        return pl.multiple_of(mine[order(g)[2]] * quarter, quarter)

    def second_at(g):
        return pl.multiple_of(mine[order(g)[2]] * quarter + mine[order(g)[3]] * shard, shard)

    def remote(g, slot, src, dst, to):
        at = g * slots + slot
        return pltpu.make_async_remote_copy(
            src_ref=src, dst_ref=dst, send_sem=ar_send.at[at], recv_sem=ar_recv.at[at],
            device_id={"lon": to[0], "lat": to[1]}, device_id_type=MESH,
        )

    def core_copies(g):
        ks = pl.ds(*PARTS[g][:2])
        return [remote(g, 0, snd0.at[ks], rcv0.at[ks], (lon, flip(lat, 1)))]

    def split_copies(g, kind, base, size, src, dst):
        ks, out = pl.ds(*PARTS[g][:2]), []
        for d in turn[kind]:
            to, place = member(kind, d)
            at = pl.ds(pl.multiple_of(place * size, size), size)
            out.append(remote(g, base + d, src.at[ks, at], dst.at[d - 1, ks], to))
        return out

    def first_copies(g):
        return split_copies(g, order(g)[2], 0, quarter, snd_a, rcv_a)

    def second_copies(g):
        return split_copies(g, order(g)[3], n_a, shard, snd_b, rcv_b)

    def beyond_copies(g):
        ks = pl.ds(*PARTS[g][:2])
        return [
            remote(g, n_a + n_b + d, rcv_c.at[beyond, ks], rcv_c.at[beyond, ks], copy_to(d))
            for d in range(1, copies)
        ]

    def gather_copies(g, kind, base, start, size):
        block = gat.at[core, pl.ds(*PARTS[g][:2]), pl.ds(start, size)]
        return [remote(g, base + d, block, block, member(kind, d)[0]) for d in turn[kind]]

    def second_gather(g):
        return gather_copies(g, order(g)[3], n_a + n_b + n_c, second_at(g), shard)

    def first_gather(g):
        return gather_copies(g, order(g)[2], n_a + 2 * n_b + n_c, first_at(g), quarter)

    def core_gather(g):
        kind, out = order(g)[2], []
        for i, d in enumerate((0,) + turn[kind]):
            came = line - d if kind == "line" else d
            place = member(kind, came)[1] if d else mine[kind]
            at = pl.ds(pl.multiple_of(place * quarter, quarter), quarter)
            block = gat.at[core, pl.ds(*PARTS[g][:2]), at]
            out.append(remote(g, slots - count[kind] + i, block, block, (lon, flip(lat, 1))))
        return out

    def start(copies_of):
        for copy in copies_of:
            copy.start()

    def wait(copies_of):
        for copy in copies_of:
            copy.wait()

    def product(g):
        k0, kn = PARTS[g][:2]
        for k in range(k0, k0 + kn):
            part = acc_m[k] + nn_dot(inp_x[...], spread_x[:, k * chans : (k + 1) * chans])
            low, high = part[:, :LANES], part[:, LANES:]
            acc[k] = jnp.where(core == 0, low, high)
            snd0[k] = jnp.where(core == 0, high, low).astype(BF16)
        start(core_copies(g))

    def k_slice(g):
        return slice(PARTS[g][0], PARTS[g][0] + PARTS[g][1])

    def core_sum(g):
        wait(core_copies(g))
        ks = k_slice(g)
        snd_a[ks] = (acc[ks] + rcv0[ks].astype(F32)).astype(BF16)
        start(first_copies(g))
        at = pl.ds(first_at(g), quarter)
        acc_a[ks] = acc[ks, at] + rcv0[ks, at].astype(F32)

    def first_sum(g):
        wait(first_copies(g))
        ks = k_slice(g)
        total = acc_a[ks]
        for d in range(count[order(g)[2]] - 1):
            total += rcv_a[d, ks].astype(F32)
        snd_b[ks] = total.astype(BF16)
        start(second_copies(g))
        acc_b[ks] = total

    def second_sum(g):
        wait(second_copies(g))
        ks = k_slice(g)
        total = acc_b[ks, pl.ds(pl.multiple_of(mine[order(g)[3]] * shard, shard), shard)]
        for d in range(count[order(g)[3]] - 1):
            total += rcv_b[d, ks].astype(F32)
        if copies > 1:
            rcv_c[beyond, ks] = total.astype(BF16)
            start(beyond_copies(g))
            wait(beyond_copies(g))
            total = rcv_c[0, ks].astype(F32)
            for d in range(1, copies):
                total += rcv_c[d, ks].astype(F32)
        gat[core, ks, pl.ds(second_at(g), shard)] = total.astype(BF16)
        start(second_gather(g))

    def second_done(g):
        wait(second_gather(g))
        start(first_gather(g))
        start(core_gather(g)[:1])

    def first_done(g):
        for got, onward in zip(first_gather(g), core_gather(g)[1:]):
            got.wait()
            onward.start()

    def core_done(g):
        wait(core_gather(g))

    def ig_part(r):
        if 0 < r < rows - 1:
            source = spread[(r - 1) * cols : r * cols, :]
        else:
            at = 0 if r == 0 else cols
            source = spread_x[at : at + cols, :]
        part = nn_dot(source, mix_v[...]).astype(BF16)
        ig_row[r] = nt_dot(eye, part).astype(BF16)

    def ig_final(b):
        part = jnp.concatenate([ig_row[r, b * group : (b + 1) * group, :] for r in range(rows)], axis=0)
        ig_v[b * chans : (b + 1) * chans, :] = nn_dot(scatter, part).astype(BF16)

    side_work = [functools.partial(ig_part, r) for r in range(rows)]
    side_work += [functools.partial(ig_final, b) for b in range(rows)]

    steps = []
    for g in range(GROUPS):
        for s, step in enumerate((core_sum, first_sum, second_sum, second_done, first_done, core_done)):
            steps.append((PACE * s + g, s, functools.partial(step, g)))
    steps.sort(key=lambda item: item[:2])

    loads[3].wait()
    for g in range(GROUPS):
        product(g)
        if g > 0 and steps[0][1] == 0:
            steps.pop(0)[2]()
    steps = [step for _, _, step in steps]
    for i, step in enumerate(steps):
        if side_work:
            side_work.pop(0)()
        step()
    for work in side_work:
        work()


def finish(scale, gat_v, ig_v, wg_hbm, out_hbm, wg_v, wg_sem, ig_sem):
    _, kernels, chans, _ = gat_v.shape
    ig_out = pltpu.make_async_copy(ig_v, out_hbm, ig_sem)
    at0 = lax.broadcasted_iota(jnp.int32, (LANES, LANES), 0)
    at1 = lax.broadcasted_iota(jnp.int32, (LANES, LANES), 1)
    eye = (at0 == at1).astype(BF16)
    ig_out.start()
    stores = []
    pieces = math.gcd(kernels, 3)
    per = kernels // pieces
    for g in range(pieces):
        for k in range(g * per, (g + 1) * per):
            for h in range(chans // LANES):
                start = k * chans + h * LANES
                wg_v[start : start + LANES, :] = nt_dot(eye, gat_v[h, k]) * scale
        rows = pl.ds(g * per * chans, per * chans)
        stores.append(pltpu.make_async_copy(wg_v.at[rows], wg_hbm.at[rows], wg_sem.at[g]))
        stores[-1].start()
    for store in stores:
        store.wait()
    ig_out.wait()


def local(nlon, nlat, inputs, cotangent, mixing, filters, support):
    chans, rows, cols = inputs.shape
    kernels = filters.shape[0]
    plane, line, copies = layout(nlon, nlat)
    quarter, shard = chans // plane, chans // (plane * line)
    slots = GROUPS * (1 + plane + 2 * (plane - 1) + 2 * (line - 1) + copies - 1)
    strip_rows = -(-(rows - 2) * 2 * LON_REACH // DEPTH) * DEPTH
    any_spec = pl.BlockSpec(memory_space=pl.ANY)
    vm = pltpu.VMEM
    flops = 2 * rows * cols * kernels * chans * chans * 3
    ig, wg = pl.pallas_call(
        functools.partial(kernel, nlon, nlat, kernels, chans, rows, cols),
        out_shape=(
            jax.ShapeDtypeStruct((chans * rows, cols), BF16),
            jax.ShapeDtypeStruct((2, kernels, chans, LANES), BF16),
        ),
        in_specs=[any_spec] * 5,
        out_specs=[pl.BlockSpec(memory_space=pltpu.VMEM)] * 2,
        scratch_shapes=[
            vm((chans * rows, cols), BF16),
            vm((chans * rows, cols), BF16),
            vm((kernels * chans, chans), BF16),
            vm((kernels * ROWS_A * rows, TAPS), BF16),
            pltpu.SMEM((rows,), jnp.int32),
            vm((rows + 2, TILE, DEPTH), BF16),
            vm((2, TILE, DEPTH), BF16),
            vm((rows, chans, cols), BF16),
            vm((chans, (rows - 2) * cols), BF16),
            vm((chans, 2 * cols + strip_rows), BF16),
            vm((rows + 2, cols + 2 * LON_REACH, chans), BF16),
            vm((rows, kernels * BLOCK, DEPTH), BF16),
            vm(((rows - 2) * cols, kernels * chans), BF16),
            vm((2 * cols + strip_rows, kernels * chans), BF16),
            vm((kernels, chans, chans), F32),
            vm((kernels, chans, LANES), F32),
            vm((kernels, chans, LANES), BF16),
            vm((kernels, chans, LANES), BF16),
            vm((kernels, chans, LANES), BF16),
            vm((kernels, quarter, LANES), F32),
            vm((plane - 1, kernels, quarter, LANES), BF16),
            vm((kernels, quarter, LANES), BF16),
            vm((kernels, quarter, LANES), F32),
            vm((line - 1, kernels, shard, LANES), BF16),
            vm((copies, kernels, shard, LANES), BF16),
            vm((rows, chans, cols), BF16),
            pltpu.SemaphoreType.DMA((5,)),
            pltpu.SemaphoreType.DMA((10,)),
            pltpu.SemaphoreType.DMA((10,)),
            pltpu.SemaphoreType.DMA((slots,)),
            pltpu.SemaphoreType.DMA((slots,)),
        ],
        compiler_params=pltpu.CompilerParams(
            collective_id=0, has_side_effects=True, vmem_limit_bytes=40 * 2**20
        ),
        cost_estimate=pl.CostEstimate(flops=flops, bytes_accessed=7 * 2**20, transcendentals=0),
    )(
        pltpu.with_memory_space_constraint(cotangent.reshape(chans * rows, cols), pltpu.HBM),
        pltpu.with_memory_space_constraint(inputs.reshape(chans * rows, cols), pltpu.HBM),
        pltpu.with_memory_space_constraint(mixing.reshape(kernels * chans, chans), pltpu.HBM),
        pltpu.with_memory_space_constraint(jnp.transpose(filters, (0, 2, 1, 3)).reshape(kernels * ROWS_A * rows, TAPS), pltpu.HBM),
        pltpu.with_memory_space_constraint(support, pltpu.HBM),
    )
    scale = 1.0 / math.sqrt(rows * nlat * cols * nlon)
    weight_grad, input_grad = pl.pallas_call(
        functools.partial(finish, scale),
        out_shape=(
            jax.ShapeDtypeStruct((kernels * chans, chans), F32),
            jax.ShapeDtypeStruct((chans * rows, cols), BF16),
        ),
        in_specs=[pl.BlockSpec(memory_space=pltpu.VMEM)] * 2,
        out_specs=(any_spec, any_spec),
        scratch_shapes=[
            vm((kernels * chans, chans), F32),
            pltpu.SemaphoreType.DMA((kernels,)),
            pltpu.SemaphoreType.DMA,
        ],
        compiler_params=pltpu.CompilerParams(vmem_limit_bytes=16 * 2**20),
    )(wg, ig)
    return input_grad.reshape(chans, rows, cols), weight_grad.reshape(kernels, chans, chans)


def solution(mesh):
    return jax.shard_map(
        functools.partial(local, mesh.shape["lon"], mesh.shape["lat"]),
        mesh=mesh,
        in_specs=(
            P(None, "lat", "lon"),
            P(None, "lat", "lon"),
            P(),
            P(None, "lat", None, None),
            P("lat"),
        ),
        out_specs=(P(None, "lat", "lon"), P()),
        check_vma=False,
    )
```

```python
import functools
import math

import jax
import jax.numpy as jnp
from jax import lax
from jax.experimental import pallas as pl
from jax.experimental.pallas import tpu as pltpu
from jax.sharding import PartitionSpec as P

LAT_REACH = 1
LON_REACH = 16
TAPS = 2 * LON_REACH + 1
ROWS_A = 2 * LAT_REACH + 1
BLOCK = 48
WINDOW = BLOCK + 2 * LON_REACH
DEPTH = 256
TILE = 16
LANES = 128
QUARTER = 4
PARTS = ((0, 2, "plane"), (2, 4, "plane"), (6, 3, "line"))
GROUPS = len(PARTS)
PACE = 2

F32 = jnp.float32
BF16 = jnp.bfloat16
MESH = pl.DeviceIdType.MESH


def nt_dot(a, b):
    return lax.dot_general(a, b, (((1,), (1,)), ((), ())), preferred_element_type=F32)


def nn_dot(a, b):
    return lax.dot_general(a, b, (((1,), (0,)), ((), ())), preferred_element_type=F32)


def flip(index, step):
    return index + step - 2 * step * ((index // step) % 2)


def layout(nlon, nlat):
    copies = (nlon // (2 * QUARTER)) * (nlat // QUARTER)
    return QUARTER, QUARTER, copies


def kernel(
    nlon, nlat, kernels, chans, rows, cols,
    cot_hbm, inp_hbm, mix_hbm, filt_hbm, support_hbm, ig_v, gat,
    cot_v, inp_v, mix_v, filt_v, support, taps_v, taps_x, by_row, inp_m, inp_x, cot_t, toep, spread, spread_x,
    acc_m, acc, snd0, rcv0, snd_a, acc_a, rcv_a, snd_b, acc_b, rcv_b, rcv_c, ig_row,
    in_sem, halo_send, halo_recv, ar_send, ar_recv,
):
    lon, lat = lax.axis_index("lon"), lax.axis_index("lat")
    core = lat % 2
    plane, line, copies = layout(nlon, nlat)

    loads = [
        pltpu.make_async_copy(cot_hbm, cot_v, in_sem.at[0]),
        pltpu.make_async_copy(filt_hbm, filt_v, in_sem.at[1]),
        pltpu.make_async_copy(inp_hbm, inp_v, in_sem.at[2]),
        pltpu.make_async_copy(mix_hbm, mix_v, in_sem.at[3]),
        pltpu.make_async_copy(support_hbm, support, in_sem.at[4]),
    ]
    lon_down, lon_up = (lon + nlon - 1) % nlon, (lon + 1) % nlon
    has_above, has_below = lat > 0, lat < nlat - 1

    x, y = lon % 2, (lat // 2) % 2
    z = (lon // 2) % line
    beyond = (lon // (2 * line)) * (nlat // 4) + lat // 4

    def plane_to(d):
        return (flip(lon, 1) if d % 2 else lon), (flip(lat, 2) if d // 2 else lat)

    def line_to(d):
        return lon + 2 * ((z + d) % line - z), lat

    def copy_to(d):
        to = (beyond + d) % copies
        lon_to = (to // (nlat // 4)) * (2 * line) + lon % (2 * line)
        return lon_to, (to % (nlat // 4)) * 4 + lat % 4

    barrier = pltpu.get_barrier_semaphore()

    def greet(lon_to, lat_to):
        pl.semaphore_signal(
            barrier, inc=1, device_id={"lon": lon_to, "lat": lat_to}, device_id_type=MESH
        )

    partners = [plane_to(d) for d in range(1, plane)] + [line_to(d) for d in range(1, line)]
    partners += [copy_to(d) for d in range(1, copies)]

    greet(lon_down, lat)
    greet(lon_up, lat)

    @pl.when(has_above)
    def _():
        for lon_to in (lon_down, lon, lon_up):
            greet(lon_to, lat - 1)

    @pl.when(has_below)
    def _():
        for lon_to in (lon_down, lon, lon_up):
            greet(lon_to, lat + 1)

    for lon_to, lat_to in partners:
        greet(lon_to, lat_to)

    for load in loads:
        load.start()

    at0 = lax.broadcasted_iota(jnp.int32, (chans, chans), 0)
    at1 = lax.broadcasted_iota(jnp.int32, (chans, chans), 1)
    group = chans // rows
    eye = (at0 == at1).astype(BF16)
    gather = (at1 == (at0 % group) * rows + at0 // group).astype(BF16)
    scatter = (at0 == (at1 % group) * rows + at1 // group).astype(BF16)

    loads[1].wait()
    loads[4].wait()
    filt_rows = kernels * ROWS_A * rows
    lane = lax.broadcasted_iota(jnp.int32, (rows, TAPS), 1)
    sub = lax.broadcasted_iota(jnp.int32, (rows, TAPS), 0)
    reach = jnp.zeros((rows, TAPS), jnp.int32)
    for r in range(rows):
        reach = jnp.where(sub == r, support[r], reach)
    keep = (jnp.abs(lane - LON_REACH) <= reach).astype(F32)
    coefs = filt_v[...].astype(F32).reshape(kernels * ROWS_A, rows, TAPS) * keep[None]
    coefs = coefs.reshape(filt_rows, TAPS).astype(BF16)
    out_rows = (rows + 2) * TILE
    pick0 = lax.broadcasted_iota(jnp.int32, (out_rows, filt_rows), 0)
    pick1 = lax.broadcasted_iota(jnp.int32, (out_rows, filt_rows), 1)
    tap = lax.broadcasted_iota(jnp.int32, (TAPS, DEPTH), 0)
    spot = lax.broadcasted_iota(jnp.int32, (TAPS, DEPTH), 1)
    placed = jnp.zeros((out_rows, DEPTH), F32)
    for a in range(ROWS_A):
        row = pick0 // TILE - a
        k = pick0 % TILE
        pick = (pick1 == k * (ROWS_A * rows) + a * rows + row) & (row >= 0) & (row < rows) & (k < kernels)
        chosen = nn_dot(pick.astype(BF16), coefs).astype(BF16)
        placed += nn_dot(chosen, (spot == a * WINDOW + TAPS - 1 - tap).astype(BF16))
    taps_v[...] = placed.astype(BF16).reshape(rows + 2, TILE, DEPTH)

    @pl.when(jnp.logical_not(has_above))
    def _():
        cot_t[0] = jnp.zeros_like(cot_t[0])
        taps_x[0] = jnp.zeros_like(taps_x[0])

    @pl.when(jnp.logical_not(has_below))
    def _():
        cot_t[rows + 1] = jnp.zeros_like(cot_t[rows + 1])
        taps_x[1] = jnp.zeros_like(taps_x[1])

    loads[0].wait()
    for b in range(rows):
        part = nn_dot(gather, cot_v[b * chans : (b + 1) * chans, :]).astype(BF16)
        for r in range(rows):
            by_row[r, b * group : (b + 1) * group, :] = part[r * group : (r + 1) * group]
    for r in range(rows):
        cot_t[r + 1, LON_REACH : LON_REACH + cols, :] = nt_dot(eye, by_row[r]).astype(BF16)

    def widen(r, more=None):
        base = taps_v[r + 1].astype(F32)
        if more is not None:
            base += taps_x[more].astype(F32)
        for k in range(kernels):
            flat = jnp.broadcast_to(base[k : k + 1], (BLOCK, DEPTH))
            toep[r, k * BLOCK : (k + 1) * BLOCK, :] = pltpu.roll(
                flat, 0, 1, stride=1, stride_axis=0
            ).astype(BF16)

    reach_out = LON_REACH
    strips = [(0, 0, reach_out), (cols - BLOCK, BLOCK - reach_out, reach_out)]
    both = 2 * reach_out
    strip_rows = spread_x.shape[0] - 2 * cols
    middle = rows - 2
    for r in range(middle):
        for at in (r * cols, (r + 1) * cols - reach_out):
            spread[at : at + reach_out, :] = jnp.zeros((reach_out, kernels * chans), BF16)
    spare = strip_rows - middle * both
    if spare:
        spread_x[2 * cols + middle * both :, :] = jnp.zeros((spare, kernels * chans), BF16)

    loads[2].wait()
    for b in range(rows):
        part = nn_dot(gather, inp_v[b * chans : (b + 1) * chans, :]).astype(BF16)
        own_rows = slice(b * group, (b + 1) * group)
        for r in range(rows):
            piece = part[r * group : (r + 1) * group]
            if 0 < r < rows - 1:
                inp_m[own_rows, (r - 1) * cols : r * cols] = piece
            else:
                at = 0 if r == 0 else cols
                inp_x[own_rows, at : at + cols] = piece
    strip0 = lax.broadcasted_iota(jnp.int32, (cols, strip_rows), 0)
    strip1 = lax.broadcasted_iota(jnp.int32, (cols, strip_rows), 1)
    chosen = jnp.zeros((chans, strip_rows), F32)
    for r in range(middle):
        lead = (strip0 < reach_out) & (strip1 == strip0 + r * both)
        trail = (strip0 >= cols - reach_out) & (strip1 == strip0 + (r * both + both - cols))
        chosen += nn_dot(inp_m[:, r * cols : (r + 1) * cols], (lead | trail).astype(BF16))
    inp_x[:, 2 * cols :] = chosen.astype(BF16)

    pad = jnp.zeros((DEPTH - ROWS_A * WINDOW, chans), BF16)

    def spread_block(r, start, low, size):
        source = jnp.concatenate(
            [cot_t[r + 2 - a, start : start + WINDOW, :] for a in range(ROWS_A)] + [pad], axis=0
        )
        if size == BLOCK:
            bands = toep[r]
        else:
            bands = jnp.concatenate(
                [toep[r, k * BLOCK + low : k * BLOCK + low + size, :] for k in range(kernels)], axis=0
            )
        return nn_dot(bands, source).astype(BF16)

    def put(ref, at, out, size):
        for k in range(kernels):
            ref[pl.ds(at, size), k * chans : (k + 1) * chans] = out[k * size : (k + 1) * size]

    def cover(first, last):
        out = [(at, 0, BLOCK) for at in range(first, last - BLOCK + 1, BLOCK)]
        rest = (last - first) % BLOCK
        if rest:
            out.append((last - BLOCK, BLOCK - rest, rest))
        return out

    edges = has_above.astype(jnp.int32) + has_below.astype(jnp.int32)
    pl.semaphore_wait(barrier, 2 + len(partners) + 3 * edges)

    own = pl.ds(LON_REACH, cols)
    head, tail = pl.ds(LON_REACH, LON_REACH), pl.ds(cols, LON_REACH)
    left, right = pl.ds(0, LON_REACH), pl.ds(LON_REACH + cols, LON_REACH)
    every = pl.ds(1, rows)

    def halo(i, src, dst, lon_to, lat_to):
        return pltpu.make_async_remote_copy(
            src_ref=src, dst_ref=dst, send_sem=halo_send.at[i], recv_sem=halo_recv.at[i],
            device_id={"lon": lon_to, "lat": lat_to}, device_id_type=MESH,
        )

    sides = [
        halo(0, cot_t.at[every, head], cot_t.at[every, right], lon_down, lat),
        halo(1, cot_t.at[every, tail], cot_t.at[every, left], lon_up, lat),
    ]
    above, below = lat - 1, lat + 1
    upward = [
        halo(2, cot_t.at[1, own], cot_t.at[rows + 1, own], lon, above),
        halo(3, cot_t.at[1, head], cot_t.at[rows + 1, right], lon_down, above),
        halo(4, cot_t.at[1, tail], cot_t.at[rows + 1, left], lon_up, above),
        halo(5, taps_v.at[0], taps_x.at[1], lon, above),
    ]
    downward = [
        halo(6, cot_t.at[rows, own], cot_t.at[0, own], lon, below),
        halo(7, cot_t.at[rows, head], cot_t.at[0, right], lon_down, below),
        halo(8, cot_t.at[rows, tail], cot_t.at[0, left], lon_up, below),
        halo(9, taps_v.at[rows + 1], taps_x.at[0], lon, below),
    ]

    for copy in sides:
        copy.start()

    @pl.when(has_above)
    def _():
        for copy in upward:
            copy.start()

    @pl.when(has_below)
    def _():
        for copy in downward:
            copy.start()

    def inner_row(r, carry):
        widen(r)
        base = pl.multiple_of((r - 1) * cols, cols)
        for start, low, size in cover(reach_out, cols - reach_out):
            put(spread, base + start + low, spread_block(r, start, low, size), size)
        return carry

    lax.fori_loop(1, rows - 1, inner_row, 0)

    for k in range(kernels):
        acc_m[k] = nn_dot(inp_m[...], spread[:, k * chans : (k + 1) * chans])

    for copy in sides:
        copy.wait()

    def side_row(r, carry):
        base = pl.multiple_of((r - 1) * cols, cols)
        base_x = pl.multiple_of(2 * cols + (r - 1) * both, both)
        for i, (start, low, size) in enumerate(strips):
            out = spread_block(r, start, low, size)
            put(spread, base + start + low, out, size)
            put(spread_x, base_x + i * size, out, size)
        return carry

    lax.fori_loop(1, rows - 1, side_row, 0)

    @pl.when(has_above)
    def _():
        for copy in upward:
            copy.wait_send()
        for copy in downward:
            copy.wait_recv()

    @pl.when(has_below)
    def _():
        for copy in downward:
            copy.wait_send()
        for copy in upward:
            copy.wait_recv()

    widen(0, 0)
    widen(rows - 1, 1)

    def end_row(i, carry):
        base = pl.multiple_of(i * cols, cols)
        for start, low, size in cover(0, cols):
            put(spread_x, base + start + low, spread_block(i * (rows - 1), start, low, size), size)
        return carry

    lax.fori_loop(0, 2, end_row, 0)

    quarter, shard = chans // plane, chans // (plane * line)
    count = {"plane": plane, "line": line}
    turn = {"plane": (3, 1, 2), "line": (2, 1, 3)}
    mine = {"plane": x * 2 + y, "line": z}
    n_a, n_b, n_c = plane - 1, line - 1, copies - 1
    slots = 1 + plane + 2 * n_a + 2 * n_b + n_c

    def member(kind, d):
        if kind == "line":
            return line_to(d), (z + d) % line
        x_to = flip(x, 1) if d % 2 else x
        y_to = flip(y, 1) if d // 2 else y
        return plane_to(d), x_to * 2 + y_to

    def order(g):
        k0, kn, one = PARTS[g]
        return k0, kn, one, ("line" if one == "plane" else "plane")

    def first_at(g):
        return pl.multiple_of(mine[order(g)[2]] * quarter, quarter)

    def second_at(g):
        return pl.multiple_of(mine[order(g)[2]] * quarter + mine[order(g)[3]] * shard, shard)

    def remote(g, slot, src, dst, to):
        at = g * slots + slot
        return pltpu.make_async_remote_copy(
            src_ref=src, dst_ref=dst, send_sem=ar_send.at[at], recv_sem=ar_recv.at[at],
            device_id={"lon": to[0], "lat": to[1]}, device_id_type=MESH,
        )

    def core_copies(g):
        ks = pl.ds(*PARTS[g][:2])
        return [remote(g, 0, snd0.at[ks], rcv0.at[ks], (lon, flip(lat, 1)))]

    def split_copies(g, kind, base, size, src, dst):
        ks, out = pl.ds(*PARTS[g][:2]), []
        for d in turn[kind]:
            to, place = member(kind, d)
            at = pl.ds(pl.multiple_of(place * size, size), size)
            out.append(remote(g, base + d, src.at[ks, at], dst.at[d - 1, ks], to))
        return out

    def first_copies(g):
        return split_copies(g, order(g)[2], 0, quarter, snd_a, rcv_a)

    def second_copies(g):
        return split_copies(g, order(g)[3], n_a, shard, snd_b, rcv_b)

    def beyond_copies(g):
        ks = pl.ds(*PARTS[g][:2])
        return [
            remote(g, n_a + n_b + d, rcv_c.at[beyond, ks], rcv_c.at[beyond, ks], copy_to(d))
            for d in range(1, copies)
        ]

    def gather_copies(g, kind, base, start, size):
        block = gat.at[core, pl.ds(*PARTS[g][:2]), pl.ds(start, size)]
        return [remote(g, base + d, block, block, member(kind, d)[0]) for d in turn[kind]]

    def second_gather(g):
        return gather_copies(g, order(g)[3], n_a + n_b + n_c, second_at(g), shard)

    def first_gather(g):
        return gather_copies(g, order(g)[2], n_a + 2 * n_b + n_c, first_at(g), quarter)

    def core_gather(g):
        kind, out = order(g)[2], []
        for i, d in enumerate((0,) + turn[kind]):
            came = line - d if kind == "line" else d
            place = member(kind, came)[1] if d else mine[kind]
            at = pl.ds(pl.multiple_of(place * quarter, quarter), quarter)
            block = gat.at[core, pl.ds(*PARTS[g][:2]), at]
            out.append(remote(g, slots - count[kind] + i, block, block, (lon, flip(lat, 1))))
        return out

    def start(copies_of):
        for copy in copies_of:
            copy.start()

    def wait(copies_of):
        for copy in copies_of:
            copy.wait()

    def product(g):
        k0, kn = PARTS[g][:2]
        for k in range(k0, k0 + kn):
            part = acc_m[k] + nn_dot(inp_x[...], spread_x[:, k * chans : (k + 1) * chans])
            low, high = part[:, :LANES], part[:, LANES:]
            acc[k] = jnp.where(core == 0, low, high)
            snd0[k] = jnp.where(core == 0, high, low).astype(BF16)
        start(core_copies(g))

    def k_slice(g):
        return slice(PARTS[g][0], PARTS[g][0] + PARTS[g][1])

    def core_sum(g):
        wait(core_copies(g))
        ks = k_slice(g)
        snd_a[ks] = (acc[ks] + rcv0[ks].astype(F32)).astype(BF16)
        start(first_copies(g))
        at = pl.ds(first_at(g), quarter)
        acc_a[ks] = acc[ks, at] + rcv0[ks, at].astype(F32)

    def first_sum(g):
        wait(first_copies(g))
        ks = k_slice(g)
        total = acc_a[ks]
        for d in range(count[order(g)[2]] - 1):
            total += rcv_a[d, ks].astype(F32)
        snd_b[ks] = total.astype(BF16)
        start(second_copies(g))
        acc_b[ks] = total

    def second_sum(g):
        wait(second_copies(g))
        ks = k_slice(g)
        total = acc_b[ks, pl.ds(pl.multiple_of(mine[order(g)[3]] * shard, shard), shard)]
        for d in range(count[order(g)[3]] - 1):
            total += rcv_b[d, ks].astype(F32)
        if copies > 1:
            rcv_c[beyond, ks] = total.astype(BF16)
            start(beyond_copies(g))
            wait(beyond_copies(g))
            total = rcv_c[0, ks].astype(F32)
            for d in range(1, copies):
                total += rcv_c[d, ks].astype(F32)
        gat[core, ks, pl.ds(second_at(g), shard)] = total.astype(BF16)
        start(second_gather(g))

    def second_done(g):
        wait(second_gather(g))
        start(first_gather(g))
        start(core_gather(g)[:1])

    def first_done(g):
        for got, onward in zip(first_gather(g), core_gather(g)[1:]):
            got.wait()
            onward.start()

    def core_done(g):
        wait(core_gather(g))

    def ig_part(r):
        if 0 < r < rows - 1:
            source = spread[(r - 1) * cols : r * cols, :]
        else:
            at = 0 if r == 0 else cols
            source = spread_x[at : at + cols, :]
        part = nn_dot(source, mix_v[...]).astype(BF16)
        ig_row[r] = nt_dot(eye, part).astype(BF16)

    def ig_final(b):
        part = jnp.concatenate([ig_row[r, b * group : (b + 1) * group, :] for r in range(rows)], axis=0)
        ig_v[b * chans : (b + 1) * chans, :] = nn_dot(scatter, part).astype(BF16)

    side_work = [functools.partial(ig_part, r) for r in range(rows)]
    side_work += [functools.partial(ig_final, b) for b in range(rows)]

    steps = []
    for g in range(GROUPS):
        for s, step in enumerate((core_sum, first_sum, second_sum, second_done, first_done, core_done)):
            steps.append((PACE * s + g, s, functools.partial(step, g)))
    steps.sort(key=lambda item: item[:2])

    loads[3].wait()
    for g in range(GROUPS):
        product(g)
        if g > 0 and steps[0][1] == 0:
            steps.pop(0)[2]()
    steps = [step for _, _, step in steps]
    for i, step in enumerate(steps):
        if side_work:
            side_work.pop(0)()
        step()
    for work in side_work:
        work()


def finish(scale, gat_v, ig_v, wg_hbm, out_hbm, wg_v, wg_sem, ig_sem):
    _, kernels, chans, _ = gat_v.shape
    ig_out = pltpu.make_async_copy(ig_v, out_hbm, ig_sem)
    at0 = lax.broadcasted_iota(jnp.int32, (LANES, LANES), 0)
    at1 = lax.broadcasted_iota(jnp.int32, (LANES, LANES), 1)
    eye = (at0 == at1).astype(BF16)
    ig_out.start()
    stores = []
    pieces = math.gcd(kernels, 3)
    per = kernels // pieces
    for g in range(pieces):
        for k in range(g * per, (g + 1) * per):
            for h in range(chans // LANES):
                start = k * chans + h * LANES
                wg_v[start : start + LANES, :] = nt_dot(eye, gat_v[h, k]) * scale
        rows = pl.ds(g * per * chans, per * chans)
        stores.append(pltpu.make_async_copy(wg_v.at[rows], wg_hbm.at[rows], wg_sem.at[g]))
        stores[-1].start()
    for store in stores:
        store.wait()
    ig_out.wait()


def local(nlon, nlat, inputs, cotangent, mixing, filters, support):
    chans, rows, cols = inputs.shape
    kernels = filters.shape[0]
    plane, line, copies = layout(nlon, nlat)
    quarter, shard = chans // plane, chans // (plane * line)
    slots = GROUPS * (1 + plane + 2 * (plane - 1) + 2 * (line - 1) + copies - 1)
    strip_rows = -(-(rows - 2) * 2 * LON_REACH // DEPTH) * DEPTH
    any_spec = pl.BlockSpec(memory_space=pl.ANY)
    vm = pltpu.VMEM
    flops = 2 * rows * cols * kernels * chans * chans * 3
    ig, wg = pl.pallas_call(
        functools.partial(kernel, nlon, nlat, kernels, chans, rows, cols),
        out_shape=(
            jax.ShapeDtypeStruct((chans * rows, cols), BF16),
            jax.ShapeDtypeStruct((2, kernels, chans, LANES), BF16),
        ),
        in_specs=[any_spec] * 5,
        out_specs=[pl.BlockSpec(memory_space=pltpu.VMEM)] * 2,
        scratch_shapes=[
            vm((chans * rows, cols), BF16),
            vm((chans * rows, cols), BF16),
            vm((kernels * chans, chans), BF16),
            vm((kernels * ROWS_A * rows, TAPS), BF16),
            pltpu.SMEM((rows,), jnp.int32),
            vm((rows + 2, TILE, DEPTH), BF16),
            vm((2, TILE, DEPTH), BF16),
            vm((rows, chans, cols), BF16),
            vm((chans, (rows - 2) * cols), BF16),
            vm((chans, 2 * cols + strip_rows), BF16),
            vm((rows + 2, cols + 2 * LON_REACH, chans), BF16),
            vm((rows, kernels * BLOCK, DEPTH), BF16),
            vm(((rows - 2) * cols, kernels * chans), BF16),
            vm((2 * cols + strip_rows, kernels * chans), BF16),
            vm((kernels, chans, chans), F32),
            vm((kernels, chans, LANES), F32),
            vm((kernels, chans, LANES), BF16),
            vm((kernels, chans, LANES), BF16),
            vm((kernels, chans, LANES), BF16),
            vm((kernels, quarter, LANES), F32),
            vm((plane - 1, kernels, quarter, LANES), BF16),
            vm((kernels, quarter, LANES), BF16),
            vm((kernels, quarter, LANES), F32),
            vm((line - 1, kernels, shard, LANES), BF16),
            vm((copies, kernels, shard, LANES), BF16),
            vm((rows, chans, cols), BF16),
            pltpu.SemaphoreType.DMA((5,)),
            pltpu.SemaphoreType.DMA((10,)),
            pltpu.SemaphoreType.DMA((10,)),
            pltpu.SemaphoreType.DMA((slots,)),
            pltpu.SemaphoreType.DMA((slots,)),
        ],
        compiler_params=pltpu.CompilerParams(
            collective_id=0, has_side_effects=True, vmem_limit_bytes=40 * 2**20
        ),
        cost_estimate=pl.CostEstimate(flops=flops, bytes_accessed=7 * 2**20, transcendentals=0),
    )(
        pltpu.with_memory_space_constraint(cotangent.reshape(chans * rows, cols), pltpu.HBM),
        pltpu.with_memory_space_constraint(inputs.reshape(chans * rows, cols), pltpu.HBM),
        pltpu.with_memory_space_constraint(mixing.reshape(kernels * chans, chans), pltpu.HBM),
        pltpu.with_memory_space_constraint(jnp.transpose(filters, (0, 2, 1, 3)).reshape(kernels * ROWS_A * rows, TAPS), pltpu.HBM),
        pltpu.with_memory_space_constraint(support, pltpu.HBM),
    )
    scale = 1.0 / math.sqrt(rows * nlat * cols * nlon)
    weight_grad, input_grad = pl.pallas_call(
        functools.partial(finish, scale),
        out_shape=(
            jax.ShapeDtypeStruct((kernels * chans, chans), F32),
            jax.ShapeDtypeStruct((chans * rows, cols), BF16),
        ),
        in_specs=[pl.BlockSpec(memory_space=pltpu.VMEM)] * 2,
        out_specs=(any_spec, any_spec),
        scratch_shapes=[
            vm((kernels * chans, chans), F32),
            pltpu.SemaphoreType.DMA((kernels,)),
            pltpu.SemaphoreType.DMA,
        ],
        compiler_params=pltpu.CompilerParams(vmem_limit_bytes=16 * 2**20),
    )(wg, ig)
    return input_grad.reshape(chans, rows, cols), weight_grad.reshape(kernels, chans, chans)


def solution(mesh):
    return jax.shard_map(
        functools.partial(local, mesh.shape["lon"], mesh.shape["lat"]),
        mesh=mesh,
        in_specs=(
            P(None, "lat", "lon"),
            P(None, "lat", "lon"),
            P(),
            P(None, "lat", None, None),
            P("lat"),
        ),
        out_specs=(P(None, "lat", "lon"), P()),
        check_vma=False,
    )
```
